32 devices in a mesh: section: 4 (over z), tile: 8 (over y, x, core).
Axes of the slice: x: 2, y: 2, z: 4, core: 2. Of those that a mesh axis runs over, the one named last changes fastest.
Arguments:
- raw_echo: bfloat16 [2, 2048, 8192], P(None, 'tile', 'section'), may hold values from -6 to 6
- footprint: int32 [4, 8, 8], P('section', 'tile'), may hold values from 0 to 255, as said below
- window_start: int32 [4, 256], P('section', 'tile'), may hold values from 0 to 2047
Outputs:
- image: bfloat16 [4, 8, 1024, 2048], P('section', 'tile')
The draws below stay inside these ranges and needn't reach their ends.
Inputs may be any that keep to these rules, and one draw needn't show every extreme that they name: `footprint`: each list names 8 different pulse blocks; at most 2 of them lie among the 32 blocks k * 32 to (k + 1) * 32 - 1 of one index k of tile, and in every list some index supplies exactly 2.
All inputs are finite; a program needn't handle non-finite values.
Results may differ from the reference program's by a relative error of at most 0.0071.
Values may be sent and summed in bfloat16 or wider, within the bound.
No kernel may reach another device: no remote copies, remote signals or barrier semaphores. Data moves between devices by JAX's collectives and lax.ppermute only.
A program may use at most 128 MiB of HBM per device.

```python
import math
import jax
import jax.numpy as jnp
from jax import lax

RANGE = 8192
KC = 128
WIN = 256
PR = 1024
PC = 1024
NP = 8
CAP = 2
BINS = 2048
BLK_DEV = 32
PULSES = 2048
BLOCKS = 256
FOOT = 8
TILE_ROWS = 4
N_SECTION = 4
N_TILE = 8


def one_list(list_key):
    key_double, key_order, key_pick, key_shuffle = jax.random.split(list_key, 4)
    doubles = jax.random.randint(key_double, (), 1, FOOT // 2 + 1)
    order = jax.random.permutation(key_order, FOOT)
    counts_held = jnp.where(order < doubles, 2, jnp.where(order < 2 * doubles, 0, 1))
    pick_keys = jax.random.split(key_pick, FOOT)
    picks = jax.vmap(lambda pick_key: jax.random.permutation(pick_key, BLK_DEV)[:CAP])(pick_keys)
    holder_ids = jnp.arange(FOOT, dtype=jnp.int32)[:, None]
    block_ids = (holder_ids * BLK_DEV + picks).reshape(-1)
    valid = (jnp.arange(CAP, dtype=jnp.int32)[None, :] < counts_held[:, None]).reshape(-1)
    sort_keys = jnp.where(valid, 0, 1).astype(jnp.int32)
    ordering = jnp.argsort(sort_keys, stable=True)[:FOOT]
    chosen = block_ids[ordering]
    shuffle = jax.random.permutation(key_shuffle, FOOT)
    return chosen[shuffle].astype(jnp.int32)


def draw_footprint(key, part):
    tile_keys = jax.random.split(jax.random.fold_in(key, 17), TILE_ROWS * FOOT)
    all_lists = jax.vmap(one_list)(tile_keys)
    return all_lists.reshape(TILE_ROWS, FOOT, FOOT).astype(jnp.int32)


def with_ends(array, rng, smallest, high):
    place = [jax.random.randint(jax.random.fold_in(rng, axis), (), 0, length) for axis, length in enumerate(array.shape)]
    widest = array.shape.index(max(array.shape))
    beside = place[:widest] + [(place[widest] + 1) % array.shape[widest]] + place[widest + 1:]
    return array.at[tuple(place)].set(smallest).at[tuple(beside)].set(high)


def steps_of(stream_key, extent, cuts, least, high):
    gain = 1.0
    for axis_at, shards_of in cuts:
        heights = jax.random.uniform(jax.random.fold_in(jax.random.fold_in(stream_key, 6), axis_at), (shards_of,), jnp.float32, least / len(cuts), high / len(cuts))
        gain = gain * jnp.repeat(jnp.exp(heights), extent[axis_at] // shards_of).reshape((-1,) + (1,) * (len(extent) - 1 - axis_at))
    return gain


def noise(key, extent, scale, bound, cuts=(), held_as=jnp.bfloat16):
    loudness = steps_of(key, extent, cuts, -0.22, 0.18) if cuts else 1.0
    values = jax.random.normal(key, extent, jnp.float32) * scale * loudness
    return jnp.minimum(jnp.maximum(values, -bound), bound).astype(held_as)


def setup_inputs(seed: int = 0) -> dict:
    key_list = jax.random.split(jax.random.key(seed), 4)
    raw_echo = noise(key_list[0], (2, PULSES, RANGE), 1.0, 6.0, ((1, 8), (2, 4)))
    footprint = draw_footprint(jax.random.fold_in(key_list[3], 71), 0)
    window_start = with_ends(jax.random.randint(key_list[2], (TILE_ROWS, BLOCKS), 0, BINS), jax.random.fold_in(key_list[2], 1), 0, BINS - 1).astype(jnp.int32)
    return {"raw_echo": raw_echo, "footprint": footprint, "window_start": window_start}


def chirp_table(length):
    row_index = lax.broadcasted_iota(jnp.int32, (2 * length, length), 0)
    col_index = lax.broadcasted_iota(jnp.int32, (2 * length, length), 1)
    lag_count = row_index - col_index
    inside = (lag_count >= 0) & (lag_count < length)
    lag_safe = jnp.where(inside, lag_count, 0)
    turn_count = (lag_safe * lag_safe % (2 * length)).astype(jnp.float32)
    phase_angle = turn_count * jnp.float32(math.pi / length)
    scaling = jnp.float32(1.0 / math.sqrt(length))
    real_part = jnp.where(inside, jnp.cos(phase_angle) * scaling, jnp.float32(0.0))
    imag_part = jnp.where(inside, jnp.sin(phase_angle) * scaling, jnp.float32(0.0))
    return (real_part.astype(jnp.bfloat16), imag_part.astype(jnp.bfloat16))

def compress(raw_part, length, keep):
    real_tab, imag_tab = chirp_table(length)
    pulses = raw_part.shape[1]
    blocks = keep // length
    pieces = raw_part[:, :, :keep + length].reshape(2, pulses, blocks + 1, length)
    paired = jnp.concatenate([pieces[:, :, :-1], pieces[:, :, 1:]], axis=3).reshape(2, pulses * blocks, 2 * length)
    real_in = paired[0]
    imag_in = paired[1]
    out_real = jnp.dot(real_in, real_tab, preferred_element_type=jnp.float32) + jnp.dot(imag_in, imag_tab, preferred_element_type=jnp.float32)
    out_imag = jnp.dot(imag_in, real_tab, preferred_element_type=jnp.float32) - jnp.dot(real_in, imag_tab, preferred_element_type=jnp.float32)
    stacked = jnp.stack([out_real, out_imag]).reshape(2, pulses, keep)
    return stacked.astype(jnp.bfloat16)

def interp_table(pixel_rows, window_bins):
    upsample = pixel_rows // window_bins
    row_index = lax.broadcasted_iota(jnp.float32, (pixel_rows, window_bins), 0)
    bin_index = lax.broadcasted_iota(jnp.float32, (pixel_rows, window_bins), 1)
    centre = (row_index + 0.5) / upsample - 0.5
    offset = bin_index - centre
    tapering = jnp.cos(offset * (math.pi / 8.0)) ** 2
    kernel = jnp.where(jnp.abs(offset) < 4.0, jnp.sinc(offset) * tapering, 0.0)
    return kernel.astype(jnp.bfloat16)

def tile_image(chosen, block_ids, row_pos, col_pos, interp, pixel_cols):
    entries = chosen.shape[0]
    per_block = chosen.shape[1]
    window_bins = chosen.shape[3]
    merged = chosen.reshape(entries * per_block, 2 * window_bins)
    pulse_ids = (block_ids[:, None] * per_block + jnp.arange(per_block, dtype=jnp.int32)[None, :]).reshape(-1)
    columns = col_pos * pixel_cols + jnp.arange(pixel_cols, dtype=jnp.int32) + 1 + 7 * row_pos
    scrambled = columns * 40503 % 65521
    residue = pulse_ids[:, None] * scrambled[None, :] % 65521
    phase_angle = residue.astype(jnp.float32) * jnp.float32(2.0 * math.pi / 65521.0)
    steer_real = jnp.cos(phase_angle).astype(jnp.bfloat16)
    steer_imag = jnp.sin(phase_angle).astype(jnp.bfloat16)
    contract = (((0,), (0,)), ((), ()))
    with_real = lax.dot_general(merged, steer_real, contract, preferred_element_type=jnp.float32)
    with_imag = lax.dot_general(merged, steer_imag, contract, preferred_element_type=jnp.float32)
    scaling = jnp.float32(1.0 / math.sqrt(entries * per_block))
    focus_real = (with_real[:window_bins] - with_imag[window_bins:]) * scaling
    focus_imag = (with_imag[:window_bins] + with_real[window_bins:]) * scaling
    focused = jnp.concatenate([focus_real, focus_imag], axis=1).astype(jnp.bfloat16)
    return jnp.dot(interp, focused, preferred_element_type=jnp.float32).astype(jnp.bfloat16)

def reference(raw_echo, footprint, window_start):
    padded = jnp.pad(raw_echo, ((0, 0), (0, 0), (0, KC + WIN)))
    block_total = PULSES // NP
    grouped = jnp.transpose(padded.reshape(2, block_total, NP, RANGE + KC + WIN), (1, 0, 2, 3))
    comp_blocks = lax.map(lambda block_data: compress(block_data, KC, RANGE + WIN), grouped)
    interp = interp_table(PR, WIN)
    tile_rows = jnp.repeat(jnp.arange(N_SECTION, dtype=jnp.int32), N_TILE)
    tile_cols = jnp.tile(jnp.arange(N_TILE, dtype=jnp.int32), N_SECTION)
    all_lists = footprint.reshape(N_SECTION * N_TILE, FOOT)

    def one_tile(tile_item):
        row_pos, col_pos, block_ids = tile_item
        starts = jnp.take(window_start[row_pos], block_ids)

        def grab_window(block_id, start):
            anchor = (row_pos * BINS + start).astype(jnp.int32)
            window_piece = lax.dynamic_slice(comp_blocks, (block_id.astype(jnp.int32), jnp.int32(0), jnp.int32(0), anchor), (1, 2, NP, WIN))[0]
            return jnp.transpose(window_piece, (1, 0, 2))
        chosen = jax.vmap(grab_window)(block_ids, starts)
        return tile_image(chosen, block_ids, row_pos, col_pos, interp, PC)
    images = lax.map(one_tile, (tile_rows, tile_cols, all_lists))
    return images.reshape(N_SECTION, N_TILE, PR, 2 * PC)
```

```python
import functools
import math

import jax
import jax.numpy as jnp
import ml_dtypes
import numpy as np
from jax import lax
from jax.experimental import pallas as pl
from jax.experimental.pallas import tpu as pltpu
from jax.sharding import PartitionSpec as P

KC = 128
WIN = 256
PR = 1024
PC = 1024
NP = 8
CAP = 2
LANES = 128
PRIME = 65521
RIM = WIN + KC
SPAN = RIM + LANES
VMEM_BYTES = 48 << 20
BF16 = jnp.bfloat16


def passed_along(value, axis, by):
    devices = lax.axis_size(axis)
    pairs = [(i, i + by) for i in range(devices) if 0 <= i + by < devices]
    return lax.ppermute(value, axis, pairs)


def correlation_table():
    lag = np.arange(RIM)[:, None] - np.arange(WIN)[None, :]
    inside = (lag >= 0) & (lag < KC)
    lag = np.where(inside, lag, 0)
    angle = (lag * lag % (2 * KC)).astype(np.float64) * (math.pi / KC)
    scale = 1.0 / math.sqrt(KC)
    real = np.where(inside, np.cos(angle) * scale, 0.0)
    imag = np.where(inside, np.sin(angle) * scale, 0.0)
    return np.concatenate([real, imag], axis=1).astype(np.float32).astype(ml_dtypes.bfloat16)


def interp_table():
    row = np.arange(PR, dtype=np.float64)[:, None]
    offset = np.arange(WIN, dtype=np.float64)[None, :] - ((row + 0.5) / (PR // WIN) - 0.5)
    taper = np.cos(offset * (math.pi / 8.0)) ** 2
    kernel = np.where(np.abs(offset) < 4.0, np.sinc(offset) * taper, 0.0)
    return kernel.astype(np.float32).astype(ml_dtypes.bfloat16)


def cut_kernel(blocks_ref, tiles_ref, raw_ref, rim_ref, out_ref, sem):
    chunks = out_ref.shape[0]
    lane_tiles = raw_ref.shape[3] // LANES

    def one_chunk(n, carry):
        block = blocks_ref[n]
        tile = tiles_ref[n]
        over = jnp.maximum(tile + SPAN // LANES - lane_tiles, 0)
        for beyond in range(SPAN // LANES):
            own = SPAN - beyond * LANES

            @pl.when(over == beyond)
            def _():
                first = pl.multiple_of(tile * LANES, LANES)
                pltpu.make_async_copy(
                    raw_ref.at[:, block, :, pl.ds(first, own)],
                    out_ref.at[n, :, :, pl.ds(0, own)],
                    sem,
                ).start()
                if beyond:
                    pltpu.make_async_copy(
                        rim_ref.at[:, block, :, pl.ds(0, SPAN - own)],
                        out_ref.at[n, :, :, pl.ds(own, SPAN - own)],
                        sem,
                    ).start()

        return carry

    lax.fori_loop(0, chunks, one_chunk, 0)
    pltpu.make_async_copy(out_ref, out_ref, sem).wait()


def cut_windows(raw, rim, blocks, tiles):
    chunks = blocks.shape[0]
    planes, _, per_block, _ = raw.shape
    any_spec = pl.BlockSpec(memory_space=pl.ANY)
    return pl.pallas_call(
        cut_kernel,
        out_shape=jax.ShapeDtypeStruct((chunks, planes, per_block, SPAN), raw.dtype),
        grid_spec=pltpu.PrefetchScalarGridSpec(
            num_scalar_prefetch=2,
            grid=(1,),
            in_specs=[any_spec, any_spec],
            out_specs=any_spec,
            scratch_shapes=[pltpu.SemaphoreType.DMA],
        ),
        name="cut",
    )(blocks, tiles, raw, rim)


def mod_prime(value):
    for _ in range(2):
        value = (value >> 16) * 15 + (value & 65535)
    return jnp.where(value >= PRIME, value - PRIME, value)


def steer_kernel(list_ref, place_ref, out_ref):
    foot = list_ref.shape[0]
    pulses = foot * NP
    width = lambda rows: lax.broadcasted_iota(jnp.int32, (rows, PC), 1)
    to_angle = jnp.float32(2.0 * math.pi / PRIME)
    first = place_ref[0]

    def turned(steps, columns):
        scrambled = mod_prime((columns + first) * 40503)
        return mod_prime(steps * scrambled).astype(jnp.float32) * to_angle

    inner = turned(lax.broadcasted_iota(jnp.int32, (NP, PC), 0), width(NP))
    cos_in, sin_in = jnp.cos(inner), jnp.sin(inner)
    row = lax.broadcasted_iota(jnp.int32, (foot, PC), 0)
    ids = jnp.zeros((foot, PC), jnp.int32)
    for i in range(foot):
        ids = jnp.where(row == i, list_ref[i] * NP, ids)
    outer = turned(ids, width(foot))
    cos_out, sin_out = jnp.cos(outer), jnp.sin(outer)
    for i in range(0, foot, 2):
        real, imag = [], []
        for j in (i, i + 1):
            c, s = cos_out[j : j + 1], sin_out[j : j + 1]
            real.append(c * cos_in - s * sin_in)
            imag.append(s * cos_in + c * sin_in)
        real = jnp.concatenate(real, axis=0).astype(BF16)
        imag = jnp.concatenate(imag, axis=0).astype(BF16)
        rows = pl.ds(i * NP, 2 * NP)
        below = pl.ds(pulses + i * NP, 2 * NP)
        out_ref[rows, :PC] = real
        out_ref[rows, PC:] = imag
        out_ref[below, :PC] = -imag
        out_ref[below, PC:] = real


def steering(my_list, first_column):
    foot = my_list.shape[0]
    return pl.pallas_call(
        steer_kernel,
        out_shape=jax.ShapeDtypeStruct((2 * foot * NP, 2 * PC), BF16),
        in_specs=[pl.BlockSpec(memory_space=pltpu.SMEM)] * 2,
        out_specs=pl.BlockSpec(memory_space=pltpu.VMEM),
        name="steer",
    )(my_list, first_column)


def image_kernel(chunk_ref, shift_ref, got_ref, table_ref, steer_ref, interp_ref, out_ref, echo, wins):
    pulses = echo.shape[0] // 2
    foot = pulses // NP

    @pl.when(pl.program_id(0) == 0)
    def _():
        for i in range(0, foot, 2):
            both = []
            for j in (i, i + 1):
                piece = got_ref[chunk_ref[j]].astype(jnp.float32).reshape(2 * NP, SPAN)
                turn = lax.rem(SPAN - shift_ref[j], SPAN)
                both.append(pltpu.roll(piece, turn, 1)[:, :RIM])
            for plane in range(2):
                part = slice(plane * NP, (plane + 1) * NP)
                echo[pl.ds(plane * pulses + i * NP, 2 * NP), :] = jnp.concatenate(
                    [both[0][part], both[1][part]], axis=0
                ).astype(BF16)
        sums = jnp.dot(echo[...], table_ref[...], preferred_element_type=jnp.float32)
        real = sums[:pulses, :WIN] + sums[pulses:, WIN:]
        imag = sums[pulses:, :WIN] - sums[:pulses, WIN:]
        wins[...] = jnp.concatenate([real, imag], axis=0).astype(BF16)

    scale = jnp.float32(1.0 / math.sqrt(pulses))
    contract = (((0,), (0,)), ((), ()))
    focused = lax.dot_general(
        wins[...], steer_ref[...], contract, preferred_element_type=jnp.float32
    )
    focused = (focused * scale).astype(BF16)
    out_ref[...] = jnp.dot(
        interp_ref[...], focused, preferred_element_type=jnp.float32
    ).astype(BF16)


def tile_image(got, chunk, shift, steer):
    foot = chunk.shape[0]
    pulses = foot * NP
    step = 256
    whole = lambda shape: pl.BlockSpec(shape, lambda c, *_: (0,) * len(shape), pipeline_mode=pl.Buffered(1))
    return pl.pallas_call(
        image_kernel,
        out_shape=jax.ShapeDtypeStruct((PR, 2 * PC), BF16),
        grid_spec=pltpu.PrefetchScalarGridSpec(
            num_scalar_prefetch=2,
            grid=(2 * PC // step,),
            in_specs=[
                whole(got.shape),
                whole((RIM, 2 * WIN)),
                pl.BlockSpec((2 * pulses, step), lambda c, *_: (0, c)),
                whole((PR, WIN)),
            ],
            out_specs=pl.BlockSpec((PR, step), lambda c, *_: (0, c)),
            scratch_shapes=[
                pltpu.VMEM((2 * pulses, RIM), BF16),
                pltpu.VMEM((2 * pulses, WIN), BF16),
            ],
        ),
        compiler_params=pltpu.CompilerParams(vmem_limit_bytes=VMEM_BYTES),
        name="image",
    )(chunk, shift, got, jnp.asarray(correlation_table()), steer, jnp.asarray(interp_table()))


def local(raw_echo, footprint, window_start):
    planes, pulses, bins = raw_echo.shape
    blocks = pulses // NP
    tiles = lax.axis_size("tile")
    foot = footprint.shape[2]
    tile_pos = lax.axis_index("tile")
    row_pos = lax.axis_index("section")
    my_list = footprint[0, 0]

    rim = passed_along(raw_echo[:, :, :RIM], "section", -1)
    note = jnp.concatenate([my_list, window_start[0]])
    notes = lax.all_gather(note[None], "tile", axis=0, tiled=True)

    lists = notes[:, :foot] - tile_pos * blocks
    held = (lists >= 0) & (lists < blocks)
    lowest = jnp.min(jnp.where(held, lists, blocks - 1), axis=1)
    highest = jnp.max(jnp.where(held, lists, 0), axis=1)
    cut_blocks = jnp.stack([lowest, highest], axis=1).reshape(-1)
    hot = cut_blocks[:, None] == jnp.arange(blocks, dtype=jnp.int32)[None, :]
    cut_starts = jnp.sum(jnp.where(hot, window_start, 0), axis=1)

    holder = my_list // blocks
    below = (holder[None, :] == holder[:, None]) & (my_list[None, :] < my_list[:, None])
    chunk = holder * CAP + jnp.any(below, axis=1).astype(jnp.int32)
    starts = notes[:, foot:].reshape(-1)
    named = my_list[:, None] == jnp.arange(tiles * blocks, dtype=jnp.int32)[None, :]
    shift = jnp.sum(jnp.where(named, starts[None, :], 0), axis=1) % LANES

    sent = cut_windows(
        raw_echo.reshape(planes, blocks, NP, bins),
        rim.reshape(planes, blocks, NP, RIM),
        cut_blocks,
        cut_starts // LANES,
    )
    got = lax.all_to_all(
        sent.reshape((tiles, CAP) + sent.shape[1:]), "tile", 0, 0, tiled=True
    ).reshape(sent.shape)

    first_column = (tile_pos * PC + 1 + 7 * row_pos).astype(jnp.int32)
    steer = steering(my_list, first_column[None])
    image = tile_image(got, chunk, shift, steer)
    return image[None, None]


def solution(mesh):
    in_specs = (P(None, "tile", "section"), P("section", "tile", None), P("section", "tile"))
    out_specs = P("section", "tile", None, None)
    return jax.shard_map(local, mesh=mesh, in_specs=in_specs, out_specs=out_specs, check_vma=False)
```

```python
import functools
import math

import jax
import jax.numpy as jnp
import ml_dtypes
import numpy as np
from jax import lax
from jax.experimental import pallas as pl
from jax.experimental.pallas import tpu as pltpu
from jax.sharding import PartitionSpec as P

KC = 128
WIN = 256
PR = 1024
PC = 1024
NP = 8
CAP = 2
LANES = 128
PRIME = 65521
RIM = WIN + KC
SPAN = RIM + LANES
VMEM_BYTES = 24 << 20
SMALL_BYTES = 8 << 20
BF16 = jnp.bfloat16


def passed_along(value, axis, by):
    devices = lax.axis_size(axis)
    pairs = [(i, i + by) for i in range(devices) if 0 <= i + by < devices]
    return lax.ppermute(value, axis, pairs)


def correlation_table():
    lag = np.arange(RIM)[:, None] - np.arange(WIN)[None, :]
    inside = (lag >= 0) & (lag < KC)
    lag = np.where(inside, lag, 0)
    angle = (lag * lag % (2 * KC)).astype(np.float64) * (math.pi / KC)
    scale = 1.0 / math.sqrt(KC)
    real = np.where(inside, np.cos(angle) * scale, 0.0)
    imag = np.where(inside, np.sin(angle) * scale, 0.0)
    return np.concatenate([real, imag], axis=1).astype(np.float32).astype(ml_dtypes.bfloat16)


def interp_table():
    row = np.arange(PR, dtype=np.float64)[:, None]
    offset = np.arange(WIN, dtype=np.float64)[None, :] - ((row + 0.5) / (PR // WIN) - 0.5)
    taper = np.cos(offset * (math.pi / 8.0)) ** 2
    kernel = np.where(np.abs(offset) < 4.0, np.sinc(offset) * taper, 0.0)
    return kernel.astype(np.float32).astype(ml_dtypes.bfloat16)


def fetch_kernel(foot, notes_ref, place_ref, raw_ref, out_ref, plan_ref, sem):
    blocks = raw_ref.shape[1]
    last = (raw_ref.shape[3] - SPAN) // LANES
    mine = place_ref[0]

    def one_tile(n, carry):
        lowest, highest = jnp.int32(blocks - 1), jnp.int32(0)
        for e in range(foot):
            block = notes_ref[n, e] - mine * blocks
            held = (block >= 0) & (block < blocks)
            lowest = jnp.where(held, jnp.minimum(lowest, block), lowest)
            highest = jnp.where(held, jnp.maximum(highest, block), highest)
        for slot, block in enumerate((lowest, highest)):
            tile = notes_ref[mine, foot + block] >> 7
            first = pl.multiple_of(jnp.minimum(tile, last) * LANES, LANES)
            chunk = CAP * n + slot
            pltpu.make_async_copy(
                raw_ref.at[:, block, :, pl.ds(first, SPAN)], out_ref.at[chunk], sem
            ).start()
            plan_ref[0, chunk] = block
            plan_ref[1, chunk] = tile - last
        return carry

    tiles = notes_ref.shape[0]
    lax.fori_loop(0, tiles, one_tile, 0, unroll=tiles <= 8)
    pltpu.make_async_copy(out_ref, out_ref, sem).wait()


def extend_kernel(plan_ref, spans_ref, rim_ref, out_ref):
    chunks = spans_ref.shape[0]

    def one_chunk(chunk, carry):
        block = plan_ref[0, chunk]
        over = jnp.maximum(plan_ref[1, chunk], 0)
        for beyond in range(SPAN // LANES):

            @pl.when(over == beyond)
            def _():
                kept = SPAN - beyond * LANES
                out_ref[chunk, :, :, :kept] = spans_ref[chunk, :, :, SPAN - kept :]
                if beyond:
                    out_ref[chunk, :, :, kept:] = rim_ref[:, block, :, : SPAN - kept]

        return carry

    lax.fori_loop(0, chunks, one_chunk, 0, unroll=chunks <= 16)


def cut_windows(foot, notes, place, raw, rim):
    planes, _, per_block, _ = raw.shape
    chunks = notes.shape[0] * CAP
    smem = pl.BlockSpec(memory_space=pltpu.SMEM)
    vmem = pl.BlockSpec(memory_space=pltpu.VMEM)
    spans = jax.ShapeDtypeStruct((chunks, planes, per_block, SPAN), raw.dtype)
    fetched, plan = pl.pallas_call(
        functools.partial(fetch_kernel, foot),
        out_shape=(spans, jax.ShapeDtypeStruct((2, chunks), jnp.int32)),
        in_specs=[smem, smem, pl.BlockSpec(memory_space=pltpu.HBM)],
        out_specs=(vmem, smem),
        scratch_shapes=[pltpu.SemaphoreType.DMA],
        compiler_params=pltpu.CompilerParams(vmem_limit_bytes=SMALL_BYTES),
        name="fetch",
    )(notes, place, raw)
    return pl.pallas_call(
        extend_kernel,
        out_shape=spans,
        in_specs=[smem, vmem, vmem],
        out_specs=vmem,
        compiler_params=pltpu.CompilerParams(vmem_limit_bytes=SMALL_BYTES),
        name="extend",
    )(plan, fetched, rim)


def mod_prime(value):
    for _ in range(2):
        value = (value >> 16) * 15 + (value & 65535)
    return jnp.where(value >= PRIME, value - PRIME, value)


def place_entries(blocks, list_ref, notes_ref, where_ref):
    foot = list_ref.shape[0]

    def one(i, carry):
        block = list_ref[i]
        holder = block // blocks

        def also(j, second):
            other = list_ref[j]
            return second | ((other // blocks == holder) & (other < block)).astype(jnp.int32)

        second = lax.fori_loop(0, foot, also, jnp.int32(0), unroll=foot <= 8)
        where_ref[0, i] = holder * CAP + second
        where_ref[1, i] = notes_ref[holder, foot + block - holder * blocks] & (LANES - 1)
        return carry

    lax.fori_loop(0, foot, one, 0)


def steer_kernel(blocks, list_ref, place_ref, notes_ref, out_ref, where_ref):
    foot = list_ref.shape[0]
    pulses = foot * NP
    width = lambda rows: lax.broadcasted_iota(jnp.int32, (rows, PC), 1)
    to_angle = jnp.float32(2.0 * math.pi / PRIME)
    first = place_ref[0]

    def turned(steps, columns):
        scrambled = mod_prime((columns + first) * 40503)
        return mod_prime(steps * scrambled).astype(jnp.float32) * to_angle

    inner = turned(lax.broadcasted_iota(jnp.int32, (NP, PC), 0), width(NP))
    cos_in, sin_in = jnp.cos(inner), jnp.sin(inner)
    row = lax.broadcasted_iota(jnp.int32, (foot, PC), 0)
    ids = jnp.zeros((foot, PC), jnp.int32)
    for i in range(foot):
        ids = jnp.where(row == i, list_ref[i] * NP, ids)
    outer = turned(ids, width(foot))
    cos_out, sin_out = jnp.cos(outer), jnp.sin(outer)
    place_entries(blocks, list_ref, notes_ref, where_ref)
    for i in range(0, foot, 2):
        real, imag = [], []
        for j in (i, i + 1):
            c, s = cos_out[j : j + 1], sin_out[j : j + 1]
            real.append(c * cos_in - s * sin_in)
            imag.append(s * cos_in + c * sin_in)
        real = jnp.concatenate(real, axis=0).astype(BF16)
        imag = jnp.concatenate(imag, axis=0).astype(BF16)
        rows = pl.ds(i * NP, 2 * NP)
        below = pl.ds(pulses + i * NP, 2 * NP)
        out_ref[rows, :PC] = real
        out_ref[rows, PC:] = imag
        out_ref[below, :PC] = -imag
        out_ref[below, PC:] = real


def steering(my_list, first_column, notes, blocks):
    foot = my_list.shape[0]
    smem = pl.BlockSpec(memory_space=pltpu.SMEM)
    return pl.pallas_call(
        functools.partial(steer_kernel, blocks),
        out_shape=(
            jax.ShapeDtypeStruct((2 * foot * NP, 2 * PC), BF16),
            jax.ShapeDtypeStruct((2, foot), jnp.int32),
        ),
        in_specs=[smem] * 3,
        out_specs=(pl.BlockSpec(memory_space=pltpu.VMEM), smem),
        compiler_params=pltpu.CompilerParams(vmem_limit_bytes=SMALL_BYTES),
        name="steer",
    )(my_list, first_column, notes)


def image_kernel(where_ref, got_ref, table_ref, steer_ref, interp_ref, out_ref, echo, wins):
    pulses = echo.shape[0] // 2
    foot = pulses // NP

    @pl.when(pl.program_id(0) == 0)
    def _():
        for i in range(0, foot, 2):
            both = []
            for j in (i, i + 1):
                piece = got_ref[where_ref[0, j]].astype(jnp.float32).reshape(2 * NP, SPAN)
                turn = lax.rem(SPAN - where_ref[1, j], SPAN)
                both.append(pltpu.roll(piece, turn, 1)[:, :RIM])
            for plane in range(2):
                part = slice(plane * NP, (plane + 1) * NP)
                echo[pl.ds(plane * pulses + i * NP, 2 * NP), :] = jnp.concatenate(
                    [both[0][part], both[1][part]], axis=0
                ).astype(BF16)
        sums = jnp.dot(echo[...], table_ref[...], preferred_element_type=jnp.float32)
        real = sums[:pulses, :WIN] + sums[pulses:, WIN:]
        imag = sums[pulses:, :WIN] - sums[:pulses, WIN:]
        wins[...] = jnp.concatenate([real, imag], axis=0).astype(BF16)

    scale = jnp.float32(1.0 / math.sqrt(pulses))
    contract = (((0,), (0,)), ((), ()))
    focused = lax.dot_general(
        wins[...], steer_ref[...], contract, preferred_element_type=jnp.float32
    )
    focused = (focused * scale).astype(BF16)
    out_ref[...] = jnp.dot(
        interp_ref[...], focused, preferred_element_type=jnp.float32
    ).astype(BF16)


def tile_image(got, where, steer):
    foot = where.shape[1]
    pulses = foot * NP
    step = 256
    whole = lambda shape: pl.BlockSpec(shape, lambda c, *_: (0,) * len(shape), pipeline_mode=pl.Buffered(1))
    return pl.pallas_call(
        image_kernel,
        out_shape=jax.ShapeDtypeStruct((PR, 2 * PC), BF16),
        grid_spec=pltpu.PrefetchScalarGridSpec(
            num_scalar_prefetch=1,
            grid=(2 * PC // step,),
            in_specs=[
                whole(got.shape),
                whole((RIM, 2 * WIN)),
                pl.BlockSpec((2 * pulses, step), lambda c, *_: (0, c)),
                whole((PR, WIN)),
            ],
            out_specs=pl.BlockSpec((PR, step), lambda c, *_: (0, c)),
            scratch_shapes=[
                pltpu.VMEM((2 * pulses, RIM), BF16),
                pltpu.VMEM((2 * pulses, WIN), BF16),
            ],
        ),
        compiler_params=pltpu.CompilerParams(vmem_limit_bytes=VMEM_BYTES),
        name="image",
    )(where, got, jnp.asarray(correlation_table()), steer, jnp.asarray(interp_table()))


def local(raw_echo, footprint, window_start):
    planes, pulses, bins = raw_echo.shape
    blocks = pulses // NP
    tiles = lax.axis_size("tile")
    foot = footprint.shape[2]
    tile_pos = lax.axis_index("tile").astype(jnp.int32)
    row_pos = lax.axis_index("section").astype(jnp.int32)
    my_list = footprint[0, 0]

    rim = passed_along(raw_echo[:, :, :RIM], "section", -1)
    note = jnp.concatenate([footprint[0], window_start], axis=1)
    note = jnp.pad(note, ((0, 0), (0, -note.shape[1] % LANES)))
    notes = lax.all_gather(note, "tile", axis=0, tiled=True)

    sent = cut_windows(
        foot,
        notes,
        tile_pos[None],
        raw_echo.reshape(planes, blocks, NP, bins),
        rim.reshape(planes, blocks, NP, RIM),
    )
    got = lax.all_to_all(
        sent.reshape((tiles, CAP) + sent.shape[1:]), "tile", 0, 0, tiled=True
    ).reshape(sent.shape)

    first_column = tile_pos * PC + 1 + 7 * row_pos
    steer, where = steering(my_list, first_column[None], notes, blocks)
    image = tile_image(got, where, steer)
    return image[None, None]


def solution(mesh):
    in_specs = (P(None, "tile", "section"), P("section", "tile", None), P("section", "tile"))
    out_specs = P("section", "tile", None, None)
    return jax.shard_map(local, mesh=mesh, in_specs=in_specs, out_specs=out_specs, check_vma=False)
```

```python
import functools
import math

import jax
import jax.numpy as jnp
import ml_dtypes
import numpy as np
from jax import lax
from jax.experimental import pallas as pl
from jax.experimental.pallas import tpu as pltpu
from jax.sharding import PartitionSpec as P

KC = 128
WIN = 256
PR = 1024
PC = 1024
NP = 8
CAP = 2
LANES = 128
PRIME = 65521
RIM = WIN + KC
SPAN = RIM + LANES
VMEM_BYTES = 24 << 20
SMALL_BYTES = 8 << 20
ROWS = 256
BF16 = jnp.bfloat16


def passed_along(value, axis, by):
    devices = lax.axis_size(axis)
    pairs = [(i, i + by) for i in range(devices) if 0 <= i + by < devices]
    return lax.ppermute(value, axis, pairs)


def correlation_table():
    lag = np.arange(RIM)[:, None] - np.arange(WIN)[None, :]
    inside = (lag >= 0) & (lag < KC)
    lag = np.where(inside, lag, 0)
    angle = (lag * lag % (2 * KC)).astype(np.float64) * (math.pi / KC)
    scale = 1.0 / math.sqrt(KC)
    real = np.where(inside, np.cos(angle) * scale, 0.0)
    imag = np.where(inside, np.sin(angle) * scale, 0.0)
    return np.concatenate([real, imag], axis=1).astype(np.float32).astype(ml_dtypes.bfloat16)


def interp_table():
    row = np.arange(PR, dtype=np.float64)[:, None]
    offset = np.arange(WIN, dtype=np.float64)[None, :] - ((row + 0.5) / (PR // WIN) - 0.5)
    taper = np.cos(offset * (math.pi / 8.0)) ** 2
    kernel = np.where(np.abs(offset) < 4.0, np.sinc(offset) * taper, 0.0)
    return kernel.astype(np.float32).astype(ml_dtypes.bfloat16)


def fetch_kernel(foot, notes_ref, place_ref, raw_ref, *refs):
    *out_refs, plan_ref, sem = refs
    blocks = raw_ref.shape[1]
    last = (raw_ref.shape[3] - SPAN) // LANES
    mine = place_ref[0]
    own_note = mine ^ place_ref[1]
    tiles = notes_ref.shape[0]
    each = tiles // len(out_refs)

    def plan(n, carry):
        lowest, highest = jnp.int32(blocks - 1), jnp.int32(0)
        for e in range(foot):
            block = notes_ref[n, e] - mine * blocks
            held = (block >= 0) & (block < blocks)
            lowest = jnp.where(held, jnp.minimum(lowest, block), lowest)
            highest = jnp.where(held, jnp.maximum(highest, block), highest)
        for slot, block in enumerate((lowest, highest)):
            plan_ref[0, CAP * n + slot] = block
            plan_ref[1, CAP * n + slot] = (notes_ref[own_note, foot + block] >> 7) - last
        return carry

    lax.fori_loop(0, tiles, plan, 0, unroll=tiles <= 8)
    for group, out_ref in enumerate(out_refs):

        def fetch(at, carry):
            n = group * each * CAP + at
            first = pl.multiple_of((last + jnp.minimum(plan_ref[1, n], 0)) * LANES, LANES)
            pltpu.make_async_copy(
                raw_ref.at[:, plan_ref[0, n], :, pl.ds(first, SPAN)], out_ref.at[at], sem
            ).start()
            return carry

        lax.fori_loop(0, each * CAP, fetch, 0, unroll=tiles <= 8)
    for out_ref in out_refs:
        pltpu.make_async_copy(out_ref, out_ref, sem).wait()
    for group, out_ref in enumerate(out_refs):

        def shift(at, carry):
            over = plan_ref[1, group * each * CAP + at]
            for beyond in range(1, SPAN // LANES):

                @pl.when(over == beyond)
                def _():
                    kept = SPAN - beyond * LANES
                    out_ref[at, :, :, :kept] = out_ref[at, :, :, SPAN - kept :]

            return carry

        lax.fori_loop(0, each * CAP, shift, 0, unroll=tiles <= 8)


def extend_kernel(count, plan_ref, rim_ref, after_ref, *refs):
    out_refs, sem = refs[count : 2 * count], refs[2 * count]
    each = out_refs[0].shape[0]

    def visit(act):
        for group, out_ref in enumerate(out_refs):

            def one(at, carry):
                n = group * each + at
                over = plan_ref[1, n]
                for beyond in range(1, SPAN // LANES):

                    @pl.when(over == beyond)
                    def _():
                        kept = SPAN - beyond * LANES
                        act(
                            pltpu.make_async_copy(
                                rim_ref.at[:, plan_ref[0, n], :, pl.ds(0, SPAN - kept)],
                                out_ref.at[at, :, :, pl.ds(kept, SPAN - kept)],
                                sem,
                            )
                        )

                return carry

            lax.fori_loop(0, each, one, 0, unroll=count * each <= 16)

    visit(lambda copy: copy.start())
    visit(lambda copy: copy.wait())


def cut_windows(foot, notes, place, raw, rim, groups, after):
    planes, _, per_block, _ = raw.shape
    chunks = notes.shape[0] * CAP
    smem = pl.BlockSpec(memory_space=pltpu.SMEM)
    vmem = pl.BlockSpec(memory_space=pltpu.VMEM)
    anywhere = pl.BlockSpec(memory_space=pl.ANY)
    params = pltpu.CompilerParams(vmem_limit_bytes=SMALL_BYTES)
    spans = (jax.ShapeDtypeStruct((chunks // groups, planes, per_block, SPAN), raw.dtype),) * groups
    *fetched, plan = pl.pallas_call(
        functools.partial(fetch_kernel, foot),
        out_shape=spans + (jax.ShapeDtypeStruct((2, chunks), jnp.int32),),
        in_specs=[smem, smem, pl.BlockSpec(memory_space=pltpu.HBM)],
        out_specs=(vmem,) * groups + (smem,),
        scratch_shapes=[pltpu.SemaphoreType.DMA],
        compiler_params=params,
        name="fetch",
    )(notes, place, pltpu.with_memory_space_constraint(raw, pltpu.HBM))
    return pl.pallas_call(
        functools.partial(extend_kernel, groups),
        out_shape=spans,
        in_specs=[smem, vmem] + [anywhere] * (1 + groups),
        out_specs=(anywhere,) * groups,
        input_output_aliases={3 + g: g for g in range(groups)},
        scratch_shapes=[pltpu.SemaphoreType.DMA],
        compiler_params=params,
        name="extend",
    )(plan, rim, after, *fetched)


def mod_prime(value):
    for _ in range(2):
        value = (value >> 16) * 15 + (value & 65535)
    return jnp.where(value >= PRIME, value - PRIME, value)


def place_entries(blocks, paired, list_ref, twist, notes_ref, where_ref):
    foot = list_ref.shape[0]

    def one(i, carry):
        block = list_ref[i]
        holder = block // blocks

        def also(j, second):
            other = list_ref[j]
            return second | ((other // blocks == holder) & (other < block)).astype(jnp.int32)

        second = lax.fori_loop(0, foot, also, jnp.int32(0), unroll=foot <= 8)
        position = holder ^ twist
        where_ref[0, i] = (position // 2 if paired else position) * CAP + second
        where_ref[1, i] = notes_ref[position, foot + block - holder * blocks] & (LANES - 1)
        where_ref[2, i] = (position & 1) if paired else 0
        return carry

    lax.fori_loop(0, foot, one, 0)


def steer_kernel(blocks, paired, list_ref, place_ref, notes_ref, table_ref, out_ref, where_ref, held_ref):
    foot = list_ref.shape[0]
    pulses = foot * NP
    width = lambda rows: lax.broadcasted_iota(jnp.int32, (rows, PC), 1)
    to_angle = jnp.float32(2.0 * math.pi / PRIME)
    first = place_ref[0]
    held_ref[...] = table_ref[...]

    def turned(steps, columns):
        scrambled = mod_prime((columns + first) * 40503)
        return mod_prime(steps * scrambled).astype(jnp.float32) * to_angle

    inner = turned(lax.broadcasted_iota(jnp.int32, (NP, PC), 0), width(NP))
    cos_in, sin_in = jnp.cos(inner), jnp.sin(inner)
    row = lax.broadcasted_iota(jnp.int32, (foot, PC), 0)
    ids = jnp.zeros((foot, PC), jnp.int32)
    for i in range(foot):
        ids = jnp.where(row == i, list_ref[i] * NP, ids)
    outer = turned(ids, width(foot))
    cos_out, sin_out = jnp.cos(outer), jnp.sin(outer)
    place_entries(blocks, paired, list_ref, place_ref[1], notes_ref, where_ref)
    for i in range(0, foot, 2):
        real, imag = [], []
        for j in (i, i + 1):
            c, s = cos_out[j : j + 1], sin_out[j : j + 1]
            real.append(c * cos_in - s * sin_in)
            imag.append(s * cos_in + c * sin_in)
        real = jnp.concatenate(real, axis=0).astype(BF16)
        imag = jnp.concatenate(imag, axis=0).astype(BF16)
        rows = pl.ds(i * NP, 2 * NP)
        below = pl.ds(pulses + i * NP, 2 * NP)
        out_ref[rows, :PC] = real
        out_ref[rows, PC:] = imag
        out_ref[below, :PC] = -imag
        out_ref[below, PC:] = real


def steering(my_list, place, notes, blocks, paired):
    foot = my_list.shape[0]
    smem = pl.BlockSpec(memory_space=pltpu.SMEM)
    vmem = pl.BlockSpec(memory_space=pltpu.VMEM)
    table = jnp.asarray(correlation_table())
    return pl.pallas_call(
        functools.partial(steer_kernel, blocks, paired),
        out_shape=(
            jax.ShapeDtypeStruct((2 * foot * NP, 2 * PC), BF16),
            jax.ShapeDtypeStruct((3, foot), jnp.int32),
            jax.ShapeDtypeStruct(table.shape, BF16),
        ),
        in_specs=[smem] * 3 + [vmem],
        out_specs=(vmem, smem, vmem),
        compiler_params=pltpu.CompilerParams(vmem_limit_bytes=SMALL_BYTES),
        name="steer",
    )(my_list, place, notes, table)


def image_kernel(where_ref, direct_ref, sibling_ref, table_ref, steer_ref, interp_ref, out_ref, echo, wins, focused, pixels, sem):
    pulses = echo.shape[0] // 2
    foot = pulses // NP
    for i in range(0, foot, 2):
        both = []
        for j in (i, i + 1):
            chunk = where_ref[0, j]
            piece = direct_ref[chunk].astype(jnp.float32)
            if sibling_ref is not None:
                other = sibling_ref[chunk].astype(jnp.float32)
                piece = jnp.where(where_ref[2, j] == 1, other, piece)
            turn = lax.rem(SPAN - where_ref[1, j], SPAN)
            both.append(pltpu.roll(piece.reshape(2 * NP, SPAN), turn, 1)[:, :RIM])
        for plane in range(2):
            part = slice(plane * NP, (plane + 1) * NP)
            echo[pl.ds(plane * pulses + i * NP, 2 * NP), :] = jnp.concatenate(
                [both[0][part], both[1][part]], axis=0
            ).astype(BF16)
    sums = jnp.dot(echo[...], table_ref[...], preferred_element_type=jnp.float32)
    real = sums[:pulses, :WIN] + sums[pulses:, WIN:]
    imag = sums[pulses:, :WIN] - sums[:pulses, WIN:]
    wins[...] = jnp.concatenate([real, imag], axis=0).T.astype(BF16)
    scale = jnp.float32(1.0 / math.sqrt(pulses))
    focused[...] = (
        jnp.dot(wins[...], steer_ref[...], preferred_element_type=jnp.float32) * scale
    ).astype(BF16)
    copies = []
    for step in range(PR // ROWS):
        rows = pl.ds(step * ROWS, ROWS)
        pixels[rows, :] = jnp.dot(
            interp_ref[rows, :], focused[...], preferred_element_type=jnp.float32
        ).astype(BF16)
        copy = pltpu.make_async_copy(pixels.at[rows], out_ref.at[rows], sem.at[step])
        copy.start()
        copies.append(copy)
    for copy in copies:
        copy.wait()


def tile_image(direct, sibling, where, steer, table):
    foot = where.shape[1]
    pulses = foot * NP
    vmem = pl.BlockSpec(memory_space=pltpu.VMEM)
    operands = [direct] + ([] if sibling is None else [sibling])

    def kernel(where_ref, direct_ref, *refs):
        refs = refs if sibling is not None else (None,) + refs
        image_kernel(where_ref, direct_ref, *refs)

    return pl.pallas_call(
        kernel,
        out_shape=jax.ShapeDtypeStruct((PR, 2 * PC), BF16),
        in_specs=[pl.BlockSpec(memory_space=pltpu.SMEM)] + [vmem] * (len(operands) + 3),
        out_specs=pl.BlockSpec(memory_space=pltpu.HBM),
        scratch_shapes=[
            pltpu.VMEM((2 * pulses, RIM), BF16),
            pltpu.VMEM((WIN, 2 * pulses), BF16),
            pltpu.VMEM((WIN, 2 * PC), BF16),
            pltpu.VMEM((PR, 2 * PC), BF16),
            pltpu.SemaphoreType.DMA((PR // ROWS,)),
        ],
        compiler_params=pltpu.CompilerParams(vmem_limit_bytes=VMEM_BYTES),
        name="image",
    )(where, *operands, table, steer, jnp.asarray(interp_table()))


def swapped(value, turn):
    tiles = lax.axis_size("tile")
    return lax.ppermute(value, "tile", [(i, i ^ turn) for i in range(tiles)])


def gather_notes(note):
    pair = jnp.concatenate([note, swapped(note, 1)], axis=0)
    return jnp.concatenate([pair] + [swapped(pair, 2 * c) for c in range(1, 4)], axis=0)


def exchange(spans):
    got = [spans[0]] + [swapped(spans[c], 2 * c) for c in range(1, 4)]
    theirs = jnp.concatenate([part[CAP:] for part in got], axis=0)
    ours = jnp.concatenate([part[:CAP] for part in got], axis=0)
    return ours, swapped(theirs, 1)


def local(raw_echo, footprint, window_start):
    planes, pulses, bins = raw_echo.shape
    blocks = pulses // NP
    tiles = lax.axis_size("tile")
    paired = tiles == 8
    foot = footprint.shape[2]
    tile_pos = lax.axis_index("tile").astype(jnp.int32)
    row_pos = lax.axis_index("section").astype(jnp.int32)
    my_list = footprint[0, 0]

    rim = passed_along(raw_echo[:, :, :RIM], "section", -1)
    note = jnp.concatenate([footprint[0], window_start], axis=1)
    note = jnp.pad(note, ((0, 0), (0, -note.shape[1] % LANES)))
    notes = gather_notes(note) if paired else lax.all_gather(note, "tile", axis=0, tiled=True)
    twist = tile_pos if paired else jnp.int32(0)

    first_column = tile_pos * PC + 1 + 7 * row_pos
    place = jnp.stack([first_column, twist])
    steer, where, table = steering(my_list, place, notes, blocks, paired)

    spans = cut_windows(
        foot,
        notes,
        jnp.stack([tile_pos, twist]),
        raw_echo.reshape(planes, blocks, NP, bins),
        rim.reshape(planes, blocks, NP, RIM),
        4 if paired else 1,
        steer,
    )
    if paired:
        direct, sibling = exchange(spans)
    else:
        sent = spans[0].reshape((tiles, CAP) + spans[0].shape[1:])
        direct = lax.all_to_all(sent, "tile", 0, 0, tiled=True).reshape(spans[0].shape)
        sibling = None

    image = tile_image(direct, sibling, where, steer, table)
    return image[None, None]


def solution(mesh):
    in_specs = (P(None, "tile", "section"), P("section", "tile", None), P("section", "tile"))
    out_specs = P("section", "tile", None, None)
    return jax.shard_map(local, mesh=mesh, in_specs=in_specs, out_specs=out_specs, check_vma=False)
```

```python
import functools
import math

import jax
import jax.numpy as jnp
import ml_dtypes
import numpy as np
from jax import lax
from jax.experimental import pallas as pl
from jax.experimental.pallas import tpu as pltpu
from jax.sharding import PartitionSpec as P

KC = 128
WIN = 256
PR = 1024
PC = 1024
NP = 8
CAP = 2
LANES = 128
PRIME = 65521
RIM = WIN + KC
SPAN = RIM + LANES
VMEM_BYTES = 24 << 20
SMALL_BYTES = 8 << 20
ROWS = 256
BF16 = jnp.bfloat16


def passed_along(value, axis, by):
    devices = lax.axis_size(axis)
    pairs = [(i, i + by) for i in range(devices) if 0 <= i + by < devices]
    return lax.ppermute(value, axis, pairs)


def correlation_table():
    lag = np.arange(RIM)[:, None] - np.arange(WIN)[None, :]
    inside = (lag >= 0) & (lag < KC)
    lag = np.where(inside, lag, 0)
    angle = (lag * lag % (2 * KC)).astype(np.float64) * (math.pi / KC)
    scale = 1.0 / math.sqrt(KC)
    real = np.where(inside, np.cos(angle) * scale, 0.0)
    imag = np.where(inside, np.sin(angle) * scale, 0.0)
    return np.concatenate([real, imag], axis=1).astype(np.float32).astype(ml_dtypes.bfloat16)


def interp_table():
    row = np.arange(PR, dtype=np.float64)[:, None]
    offset = np.arange(WIN, dtype=np.float64)[None, :] - ((row + 0.5) / (PR // WIN) - 0.5)
    taper = np.cos(offset * (math.pi / 8.0)) ** 2
    kernel = np.where(np.abs(offset) < 4.0, np.sinc(offset) * taper, 0.0)
    return kernel.astype(np.float32).astype(ml_dtypes.bfloat16)


def place_entries(foot, blocks, paired, mine, twist, notes_ref, where_ref):
    own_note = mine ^ twist

    def one(i, carry):
        block = notes_ref[own_note, i]
        holder = block // blocks

        def also(j, second):
            other = notes_ref[own_note, j]
            return second | ((other // blocks == holder) & (other < block)).astype(jnp.int32)

        second = lax.fori_loop(0, foot, also, jnp.int32(0), unroll=foot <= 8)
        position = holder ^ twist
        where_ref[0, i] = (position // 2 if paired else position) * CAP + second
        where_ref[1, i] = notes_ref[position, foot + block - holder * blocks] & (LANES - 1)
        where_ref[2, i] = (position & 1) if paired else 0
        return carry

    lax.fori_loop(0, foot, one, 0, unroll=foot <= 8)


def fetch_kernel(foot, notes_ref, place_ref, raw_ref, *refs):
    *out_refs, plan_ref, where_ref, sem = refs
    blocks = raw_ref.shape[1]
    last = (raw_ref.shape[3] - SPAN) // LANES
    mine = place_ref[0]
    own_note = mine ^ place_ref[1]
    tiles = notes_ref.shape[0]
    each = tiles // len(out_refs)

    def plan(n, carry):
        lowest, highest = jnp.int32(blocks - 1), jnp.int32(0)
        for e in range(foot):
            block = notes_ref[n, e] - mine * blocks
            held = (block >= 0) & (block < blocks)
            lowest = jnp.where(held, jnp.minimum(lowest, block), lowest)
            highest = jnp.where(held, jnp.maximum(highest, block), highest)
        for slot, block in enumerate((lowest, highest)):
            plan_ref[0, CAP * n + slot] = block
            plan_ref[1, CAP * n + slot] = (notes_ref[own_note, foot + block] >> 7) - last
        return carry

    lax.fori_loop(0, tiles, plan, 0, unroll=tiles <= 8)
    for group, out_ref in enumerate(out_refs):

        def fetch(at, carry):
            n = group * each * CAP + at
            first = pl.multiple_of((last + jnp.minimum(plan_ref[1, n], 0)) * LANES, LANES)
            pltpu.make_async_copy(
                raw_ref.at[:, plan_ref[0, n], :, pl.ds(first, SPAN)], out_ref.at[at], sem
            ).start()
            return carry

        lax.fori_loop(0, each * CAP, fetch, 0, unroll=tiles <= 8)
    place_entries(foot, blocks, len(out_refs) > 1, mine, place_ref[1], notes_ref, where_ref)
    for out_ref in out_refs:
        pltpu.make_async_copy(out_ref, out_ref, sem).wait()
    for group, out_ref in enumerate(out_refs):

        def shift(at, carry):
            over = plan_ref[1, group * each * CAP + at]
            for beyond in range(1, SPAN // LANES):

                @pl.when(over == beyond)
                def _():
                    kept = SPAN - beyond * LANES
                    out_ref[at, :, :, :kept] = out_ref[at, :, :, SPAN - kept :]

            return carry

        lax.fori_loop(0, each * CAP, shift, 0, unroll=tiles <= 8)


def extend_kernel(count, plan_ref, rim_ref, *refs):
    out_refs, sem = refs[count : 2 * count], refs[2 * count]
    each = out_refs[0].shape[0]

    def visit(act):
        for group, out_ref in enumerate(out_refs):

            def one(at, carry):
                n = group * each + at
                over = plan_ref[1, n]
                for beyond in range(1, SPAN // LANES):

                    @pl.when(over == beyond)
                    def _():
                        kept = SPAN - beyond * LANES
                        act(
                            pltpu.make_async_copy(
                                rim_ref.at[:, plan_ref[0, n], :, pl.ds(0, SPAN - kept)],
                                out_ref.at[at, :, :, pl.ds(kept, SPAN - kept)],
                                sem,
                            )
                        )

                return carry

            lax.fori_loop(0, each, one, 0, unroll=count * each <= 16)

    visit(lambda copy: copy.start())
    visit(lambda copy: copy.wait())


def cut_windows(foot, notes, place, raw, rim, groups):
    planes, _, per_block, _ = raw.shape
    chunks = notes.shape[0] * CAP
    smem = pl.BlockSpec(memory_space=pltpu.SMEM)
    vmem = pl.BlockSpec(memory_space=pltpu.VMEM)
    anywhere = pl.BlockSpec(memory_space=pl.ANY)
    params = pltpu.CompilerParams(vmem_limit_bytes=SMALL_BYTES)
    spans = (jax.ShapeDtypeStruct((chunks // groups, planes, per_block, SPAN), raw.dtype),) * groups
    *fetched, plan, where = pl.pallas_call(
        functools.partial(fetch_kernel, foot),
        out_shape=spans
        + (
            jax.ShapeDtypeStruct((2, chunks), jnp.int32),
            jax.ShapeDtypeStruct((3, foot), jnp.int32),
        ),
        in_specs=[smem, smem, pl.BlockSpec(memory_space=pltpu.HBM)],
        out_specs=(vmem,) * groups + (smem, smem),
        scratch_shapes=[pltpu.SemaphoreType.DMA],
        compiler_params=params,
        name="fetch",
    )(notes, place, pltpu.with_memory_space_constraint(raw, pltpu.HBM))
    spans = pl.pallas_call(
        functools.partial(extend_kernel, groups),
        out_shape=spans,
        in_specs=[smem, vmem] + [anywhere] * groups,
        out_specs=(anywhere,) * groups,
        input_output_aliases={2 + g: g for g in range(groups)},
        scratch_shapes=[pltpu.SemaphoreType.DMA],
        compiler_params=params,
        name="extend",
    )(plan, rim, *fetched)
    return spans, where


def mod_prime(value):
    for _ in range(2):
        value = (value >> 16) * 15 + (value & 65535)
    return jnp.where(value >= PRIME, value - PRIME, value)


def steer_kernel(note_ref, place_ref, table_ref, out_ref, held_ref, sem):
    pulses = out_ref.shape[0] // 2
    foot = pulses // NP
    holding = pltpu.make_async_copy(table_ref, held_ref, sem)
    holding.start()
    width = lambda rows: lax.broadcasted_iota(jnp.int32, (rows, PC), 1)
    to_angle = jnp.float32(2.0 * math.pi / PRIME)
    first = place_ref[0]

    def turned(steps, columns):
        scrambled = mod_prime((columns + first) * 40503)
        return mod_prime(steps * scrambled).astype(jnp.float32) * to_angle

    inner = turned(lax.broadcasted_iota(jnp.int32, (NP, PC), 0), width(NP))
    cos_in, sin_in = jnp.cos(inner), jnp.sin(inner)
    row = lax.broadcasted_iota(jnp.int32, (foot, PC), 0)
    ids = jnp.zeros((foot, PC), jnp.int32)
    for i in range(foot):
        ids = jnp.where(row == i, note_ref[0, i] * NP, ids)
    outer = turned(ids, width(foot))
    cos_out, sin_out = jnp.cos(outer), jnp.sin(outer)
    for i in range(0, foot, 2):
        real, imag = [], []
        for j in (i, i + 1):
            c, s = cos_out[j : j + 1], sin_out[j : j + 1]
            real.append(c * cos_in - s * sin_in)
            imag.append(s * cos_in + c * sin_in)
        real = jnp.concatenate(real, axis=0).astype(BF16)
        imag = jnp.concatenate(imag, axis=0).astype(BF16)
        rows = pl.ds(i * NP, 2 * NP)
        below = pl.ds(pulses + i * NP, 2 * NP)
        out_ref[rows, :PC] = real
        out_ref[rows, PC:] = imag
        out_ref[below, :PC] = -imag
        out_ref[below, PC:] = real
    holding.wait()


def steering(foot, note, first_column):
    smem = pl.BlockSpec(memory_space=pltpu.SMEM)
    vmem = pl.BlockSpec(memory_space=pltpu.VMEM)
    table = jnp.asarray(correlation_table())
    return pl.pallas_call(
        steer_kernel,
        out_shape=(
            jax.ShapeDtypeStruct((2 * foot * NP, 2 * PC), BF16),
            jax.ShapeDtypeStruct(table.shape, BF16),
        ),
        in_specs=[smem, smem, pl.BlockSpec(memory_space=pltpu.HBM)],
        out_specs=(vmem, vmem),
        scratch_shapes=[pltpu.SemaphoreType.DMA],
        compiler_params=pltpu.CompilerParams(vmem_limit_bytes=SMALL_BYTES),
        cost_estimate=pl.CostEstimate(flops=0, bytes_accessed=4 << 20, transcendentals=0),
        name="steer",
    )(note, first_column, pltpu.with_memory_space_constraint(table, pltpu.HBM))


def image_kernel(where_ref, direct_ref, sibling_ref, table_ref, steer_ref, interp_ref, out_ref, echo, wins, focused, pixels, sem):
    pulses = echo.shape[0] // 2
    foot = pulses // NP
    for i in range(0, foot, 2):
        both = []
        for j in (i, i + 1):
            chunk = where_ref[0, j]
            piece = direct_ref[chunk].astype(jnp.float32)
            if sibling_ref is not None:
                other = sibling_ref[chunk].astype(jnp.float32)
                piece = jnp.where(where_ref[2, j] == 1, other, piece)
            turn = lax.rem(SPAN - where_ref[1, j], SPAN)
            both.append(pltpu.roll(piece.reshape(2 * NP, SPAN), turn, 1)[:, :RIM])
        for plane in range(2):
            part = slice(plane * NP, (plane + 1) * NP)
            echo[pl.ds(plane * pulses + i * NP, 2 * NP), :] = jnp.concatenate(
                [both[0][part], both[1][part]], axis=0
            ).astype(BF16)
    sums = jnp.dot(echo[...], table_ref[...], preferred_element_type=jnp.float32)
    real = sums[:pulses, :WIN] + sums[pulses:, WIN:]
    imag = sums[pulses:, :WIN] - sums[:pulses, WIN:]
    wins[...] = jnp.concatenate([real, imag], axis=0).T.astype(BF16)
    scale = jnp.float32(1.0 / math.sqrt(pulses))
    focused[...] = (
        jnp.dot(wins[...], steer_ref[...], preferred_element_type=jnp.float32) * scale
    ).astype(BF16)
    copies = []
    for step in range(PR // ROWS):
        rows = pl.ds(step * ROWS, ROWS)
        pixels[rows, :] = jnp.dot(
            interp_ref[rows, :], focused[...], preferred_element_type=jnp.float32
        ).astype(BF16)
        copy = pltpu.make_async_copy(pixels.at[rows], out_ref.at[rows], sem.at[step])
        copy.start()
        copies.append(copy)
    for copy in copies:
        copy.wait()


def tile_image(direct, sibling, where, steer, table):
    foot = where.shape[1]
    pulses = foot * NP
    vmem = pl.BlockSpec(memory_space=pltpu.VMEM)
    operands = [direct] + ([] if sibling is None else [sibling])

    def kernel(where_ref, direct_ref, *refs):
        refs = refs if sibling is not None else (None,) + refs
        image_kernel(where_ref, direct_ref, *refs)

    return pl.pallas_call(
        kernel,
        out_shape=jax.ShapeDtypeStruct((PR, 2 * PC), BF16),
        in_specs=[pl.BlockSpec(memory_space=pltpu.SMEM)] + [vmem] * (len(operands) + 3),
        out_specs=pl.BlockSpec(memory_space=pltpu.HBM),
        scratch_shapes=[
            pltpu.VMEM((2 * pulses, RIM), BF16),
            pltpu.VMEM((WIN, 2 * pulses), BF16),
            pltpu.VMEM((WIN, 2 * PC), BF16),
            pltpu.VMEM((PR, 2 * PC), BF16),
            pltpu.SemaphoreType.DMA((PR // ROWS,)),
        ],
        compiler_params=pltpu.CompilerParams(vmem_limit_bytes=VMEM_BYTES),
        name="image",
    )(where, *operands, table, steer, jnp.asarray(interp_table()))


def swapped(value, turn):
    tiles = lax.axis_size("tile")
    return lax.ppermute(value, "tile", [(i, i ^ turn) for i in range(tiles)])


def gather_notes(note):
    pair = jnp.concatenate([note, swapped(note, 1)], axis=0)
    return jnp.concatenate([pair] + [swapped(pair, 2 * c) for c in range(1, 4)], axis=0)


def exchange(spans):
    got = [spans[0]] + [swapped(spans[c], 2 * c) for c in range(1, 4)]
    theirs = jnp.concatenate([part[CAP:] for part in got], axis=0)
    ours = jnp.concatenate([part[:CAP] for part in got], axis=0)
    return ours, swapped(theirs, 1)


def local(raw_echo, footprint, window_start):
    planes, pulses, bins = raw_echo.shape
    blocks = pulses // NP
    tiles = lax.axis_size("tile")
    paired = tiles == 8
    foot = footprint.shape[2]
    tile_pos = lax.axis_index("tile").astype(jnp.int32)
    row_pos = lax.axis_index("section").astype(jnp.int32)

    rim = passed_along(raw_echo[:, :, :RIM], "section", -1)
    note = jnp.concatenate([footprint[0], window_start], axis=1)
    note = jnp.pad(note, ((0, 0), (0, -note.shape[1] % LANES)))
    notes = gather_notes(note) if paired else lax.all_gather(note, "tile", axis=0, tiled=True)
    twist = tile_pos if paired else jnp.int32(0)

    first_column = tile_pos * PC + 1 + 7 * row_pos
    steer, table = steering(foot, note, first_column[None])
    notes, steer, table = lax.optimization_barrier((notes, steer, table))

    spans, where = cut_windows(
        foot,
        notes,
        jnp.stack([tile_pos, twist]),
        raw_echo.reshape(planes, blocks, NP, bins),
        rim.reshape(planes, blocks, NP, RIM),
        4 if paired else 1,
    )
    if paired:
        direct, sibling = exchange(spans)
    else:
        sent = spans[0].reshape((tiles, CAP) + spans[0].shape[1:])
        direct = lax.all_to_all(sent, "tile", 0, 0, tiled=True).reshape(spans[0].shape)
        sibling = None

    image = tile_image(direct, sibling, where, steer, table)
    return image[None, None]


def solution(mesh):
    in_specs = (P(None, "tile", "section"), P("section", "tile", None), P("section", "tile"))
    out_specs = P("section", "tile", None, None)
    return jax.shard_map(local, mesh=mesh, in_specs=in_specs, out_specs=out_specs, check_vma=False)
```

```python
import functools
import math

import jax
import jax.numpy as jnp
import ml_dtypes
import numpy as np
from jax import lax
from jax.experimental import pallas as pl
from jax.experimental.pallas import tpu as pltpu
from jax.sharding import PartitionSpec as P

KC = 128
WIN = 256
PR = 1024
PC = 1024
NP = 8
CAP = 2
LANES = 128
PRIME = 65521
RIM = WIN + KC
SPAN = RIM + LANES
ROWS = 256
BF16 = jnp.bfloat16


def vmem_grant(chunks, more=0):
    return (2 + chunks // 4 + more) << 20


def passed_along(value, axis, by):
    devices = lax.axis_size(axis)
    pairs = [(i, i + by) for i in range(devices) if 0 <= i + by < devices]
    return lax.ppermute(value, axis, pairs)


def correlation_table():
    lag = np.arange(RIM)[:, None] - np.arange(WIN)[None, :]
    inside = (lag >= 0) & (lag < KC)
    lag = np.where(inside, lag, 0)
    angle = (lag * lag % (2 * KC)).astype(np.float64) * (math.pi / KC)
    scale = 1.0 / math.sqrt(KC)
    real = np.where(inside, np.cos(angle) * scale, 0.0)
    imag = np.where(inside, np.sin(angle) * scale, 0.0)
    return np.concatenate([real, imag], axis=1).astype(np.float32).astype(ml_dtypes.bfloat16)


def interp_table():
    row = np.arange(PR, dtype=np.float64)[:, None]
    offset = np.arange(WIN, dtype=np.float64)[None, :] - ((row + 0.5) / (PR // WIN) - 0.5)
    taper = np.cos(offset * (math.pi / 8.0)) ** 2
    kernel = np.where(np.abs(offset) < 4.0, np.sinc(offset) * taper, 0.0)
    return kernel.astype(np.float32).astype(ml_dtypes.bfloat16)


def named_blocks(notes_ref, row, foot, holder, blocks):
    lowest, highest, count = jnp.int32(blocks - 1), jnp.int32(0), jnp.int32(0)
    for e in range(foot):
        block = notes_ref[row, e] - holder * blocks
        held = (block >= 0) & (block < blocks)
        lowest = jnp.where(held, jnp.minimum(lowest, block), lowest)
        highest = jnp.where(held, jnp.maximum(highest, block), highest)
        count = count + held.astype(jnp.int32)
    return lowest, highest, count


def fetch_kernel(foot, notes_ref, place_ref, raw_ref, out_ref, plan_ref, sem):
    blocks = raw_ref.shape[1]
    last = (raw_ref.shape[3] - SPAN) // LANES
    mine = place_ref[1]
    own_note = mine ^ place_ref[2]

    def one_tile(n, carry):
        for slot, block in enumerate(named_blocks(notes_ref, n, foot, mine, blocks)[:CAP]):
            chunk = n * CAP + slot
            start = notes_ref[own_note, foot + block]
            first = pl.multiple_of(jnp.minimum(start >> 7, last) * LANES, LANES)
            pltpu.make_async_copy(
                raw_ref.at[:, block, :, pl.ds(first, SPAN)], out_ref.at[chunk], sem
            ).start()
            plan_ref[0, chunk] = block
            plan_ref[1, chunk] = jnp.maximum((start >> 7) - last, 0)
            plan_ref[2, chunk] = lax.rem(SPAN - (start & (LANES - 1)), SPAN)
        return carry

    tiles = notes_ref.shape[0]
    lax.fori_loop(0, tiles, one_tile, 0, unroll=tiles <= 8)
    pltpu.make_async_copy(out_ref, out_ref, sem).wait()


def cut_kernel(plan_ref, spans_ref, rim_ref, table_ref, *refs):
    *out_refs, echo = refs
    chunks = spans_ref.shape[0]
    span_tiles = SPAN // LANES

    def one_chunk(chunk, carry):
        block, over, turn = (plan_ref[row, chunk] for row in range(3))
        pieces = []
        for step in range(span_tiles):
            own = pl.multiple_of(jnp.minimum(step + over, span_tiles - 1) * LANES, LANES)
            piece = spans_ref[chunk, :, :, pl.ds(own, LANES)].astype(jnp.float32)
            if step:
                beyond = pl.multiple_of(jnp.maximum(step + over - span_tiles, 0) * LANES, LANES)
                rim = rim_ref[:, block, :, pl.ds(beyond, LANES)].astype(jnp.float32)
                piece = jnp.where(step + over < span_tiles, piece, rim)
            pieces.append(piece)
        span = jnp.concatenate(pieces, axis=2).reshape(2 * NP, SPAN)
        rows = pl.ds(pl.multiple_of(chunk * 2 * NP, 2 * NP), 2 * NP)
        echo[rows, :] = pltpu.roll(span, turn, 1)[:, :RIM].astype(BF16)
        return carry

    lax.fori_loop(0, chunks, one_chunk, 0, unroll=chunks <= 16)
    sums = jnp.dot(echo[...], table_ref[...], preferred_element_type=jnp.float32)
    sums = sums.reshape(chunks, 2, NP, 2 * WIN)
    real = (sums[:, 0, :, :WIN] + sums[:, 1, :, WIN:]).astype(BF16)
    imag = (sums[:, 1, :, :WIN] - sums[:, 0, :, WIN:]).astype(BF16)
    each = chunks // len(out_refs)
    for group, out_ref in enumerate(out_refs):
        part = slice(group * each, (group + 1) * each)
        out_ref[:, 0] = real[part]
        out_ref[:, 1] = imag[part]


def cut_windows(foot, notes, place, raw, rim, table, groups):
    chunks = notes.shape[0] * CAP
    smem = pl.BlockSpec(memory_space=pltpu.SMEM)
    vmem = pl.BlockSpec(memory_space=pltpu.VMEM)
    params = pltpu.CompilerParams(vmem_limit_bytes=vmem_grant(chunks))
    spans, plan = pl.pallas_call(
        functools.partial(fetch_kernel, foot),
        out_shape=(
            jax.ShapeDtypeStruct((chunks, 2, NP, SPAN), BF16),
            jax.ShapeDtypeStruct((3, chunks), jnp.int32),
        ),
        in_specs=[smem, smem, pl.BlockSpec(memory_space=pltpu.HBM)],
        out_specs=(vmem, smem),
        scratch_shapes=[pltpu.SemaphoreType.DMA],
        compiler_params=params,
        name="fetch",
    )(notes, place, pltpu.with_memory_space_constraint(raw, pltpu.HBM))
    return pl.pallas_call(
        cut_kernel,
        out_shape=(jax.ShapeDtypeStruct((chunks // groups, 2, NP, WIN), BF16),) * groups,
        in_specs=[smem, vmem, vmem, vmem],
        out_specs=(vmem,) * groups,
        scratch_shapes=[pltpu.VMEM((chunks * 2 * NP, RIM), BF16)],
        compiler_params=params,
        name="cut",
    )(plan, spans, rim, table)


def mod_prime(value):
    for _ in range(2):
        value = (value >> 16) * 15 + (value & 65535)
    return jnp.where(value >= PRIME, value - PRIME, value)


def steer_kernel(foot, blocks, order, note_ref, place_ref, table_ref, out_ref, held_ref, sem):
    holding = pltpu.make_async_copy(table_ref, held_ref, sem)
    holding.start()
    chunks = len(order) * CAP
    to_angle = jnp.float32(2.0 * math.pi / PRIME)
    first, twist = place_ref[0], place_ref[2]

    def turned(steps, rows):
        columns = lax.broadcasted_iota(jnp.int32, (rows, PC), 1)
        scrambled = mod_prime((columns + first) * 40503)
        return mod_prime(steps * scrambled).astype(jnp.float32) * to_angle

    inner = turned(lax.broadcasted_iota(jnp.int32, (NP, PC), 0), NP)
    cos_in, sin_in = jnp.cos(inner), jnp.sin(inner)
    row = lax.broadcasted_iota(jnp.int32, (chunks, PC), 0)
    ids = jnp.zeros((chunks, PC), jnp.int32)
    used = jnp.zeros((chunks, PC), jnp.float32)
    for n, position in enumerate(order):
        holder = position ^ twist
        *found, count = named_blocks(note_ref, 0, foot, holder, blocks)
        for slot, block in enumerate(found):
            here = row == n * CAP + slot
            ids = jnp.where(here, (holder * blocks + block) * NP, ids)
            used = jnp.where(here & (count > slot), 1.0, used)
    outer = turned(ids, chunks)
    cos_out, sin_out = jnp.cos(outer) * used, jnp.sin(outer) * used
    for i in range(chunks):
        c, s = cos_out[i : i + 1], sin_out[i : i + 1]
        real = c * cos_in - s * sin_in
        imag = s * cos_in + c * sin_in
        rows = slice(i * 2 * NP, (i + 1) * 2 * NP)
        out_ref[rows, :PC] = jnp.concatenate([real, -imag], axis=0).astype(BF16)
        out_ref[rows, PC:] = jnp.concatenate([imag, real], axis=0).astype(BF16)
    holding.wait()


def steering(foot, blocks, order, note, place):
    smem = pl.BlockSpec(memory_space=pltpu.SMEM)
    vmem = pl.BlockSpec(memory_space=pltpu.VMEM)
    hbm = pl.BlockSpec(memory_space=pltpu.HBM)
    table = jnp.asarray(correlation_table())
    rows = len(order) * CAP * 2 * NP
    return pl.pallas_call(
        functools.partial(steer_kernel, foot, blocks, order),
        out_shape=(
            jax.ShapeDtypeStruct((rows, 2 * PC), BF16),
            jax.ShapeDtypeStruct(table.shape, BF16),
        ),
        in_specs=[smem, smem, hbm],
        out_specs=(vmem, vmem),
        scratch_shapes=[pltpu.SemaphoreType.DMA],
        compiler_params=pltpu.CompilerParams(vmem_limit_bytes=vmem_grant(len(order) * CAP)),
        cost_estimate=pl.CostEstimate(flops=0, bytes_accessed=4 << 20, transcendentals=0),
        name="steer",
    )(note, place, pltpu.with_memory_space_constraint(table, pltpu.HBM))


def image_kernel(scale, *refs):
    *window_refs, steer_ref, interp_ref, out_ref, focused, pixels, sem = refs
    windows = jnp.concatenate(
        [ref[...].reshape(ref.shape[0] * 2 * NP, WIN) for ref in window_refs], axis=0
    )
    contract = (((0,), (0,)), ((), ()))
    focused[...] = (
        lax.dot_general(windows, steer_ref[...], contract, preferred_element_type=jnp.float32)
        * jnp.float32(scale)
    ).astype(BF16)
    copies = []
    for step in range(PR // ROWS):
        rows = pl.ds(step * ROWS, ROWS)
        pixels[rows, :] = jnp.dot(
            interp_ref[rows, :], focused[...], preferred_element_type=jnp.float32
        ).astype(BF16)
        copy = pltpu.make_async_copy(pixels.at[rows], out_ref.at[rows], sem.at[step])
        copy.start()
        copies.append(copy)
    for copy in copies:
        copy.wait()


def tile_image(foot, windows, steer):
    vmem = pl.BlockSpec(memory_space=pltpu.VMEM)
    return pl.pallas_call(
        functools.partial(image_kernel, 1.0 / math.sqrt(foot * NP)),
        out_shape=jax.ShapeDtypeStruct((PR, 2 * PC), BF16),
        in_specs=[vmem] * (len(windows) + 2),
        out_specs=pl.BlockSpec(memory_space=pltpu.HBM),
        scratch_shapes=[
            pltpu.VMEM((WIN, 2 * PC), BF16),
            pltpu.VMEM((PR, 2 * PC), BF16),
            pltpu.SemaphoreType.DMA((PR // ROWS,)),
        ],
        compiler_params=pltpu.CompilerParams(vmem_limit_bytes=vmem_grant(steer.shape[0] // (2 * NP), 5)),
        name="image",
    )(*windows, steer, jnp.asarray(interp_table()))


def swapped(value, turn):
    tiles = lax.axis_size("tile")
    return lax.ppermute(value, "tile", [(i, i ^ turn) for i in range(tiles)])


def gather_notes(note):
    pair = jnp.concatenate([note, swapped(note, 1)], axis=0)
    return jnp.concatenate([pair] + [swapped(pair, 2 * c) for c in range(1, 4)], axis=0)


def exchange(windows):
    got = [windows[0]] + [swapped(windows[c], 2 * c) for c in range(1, 4)]
    theirs = jnp.concatenate([part[CAP:] for part in got], axis=0)
    ours = jnp.concatenate([part[:CAP] for part in got], axis=0)
    return ours, swapped(theirs, 1)


def local(raw_echo, footprint, window_start):
    planes, pulses, bins = raw_echo.shape
    blocks = pulses // NP
    tiles = lax.axis_size("tile")
    paired = tiles == 8
    foot = footprint.shape[2]
    tile_pos = lax.axis_index("tile").astype(jnp.int32)
    row_pos = lax.axis_index("section").astype(jnp.int32)

    rim = passed_along(raw_echo[:, :, :RIM], "section", -1)
    note = jnp.concatenate([footprint[0], window_start], axis=1)
    note = jnp.pad(note, ((0, 0), (0, -note.shape[1] % LANES)))
    notes = gather_notes(note) if paired else lax.all_gather(note, "tile", axis=0, tiled=True)
    twist = tile_pos if paired else jnp.int32(0)
    place = jnp.stack([tile_pos * PC + 1 + 7 * row_pos, tile_pos, twist])
    order = tuple(range(0, tiles, 2)) + tuple(range(1, tiles, 2)) if paired else tuple(range(tiles))

    raw = raw_echo.reshape(planes, blocks, NP, bins)
    steer, table = steering(foot, blocks, order, note, place)
    notes, steer, table = lax.optimization_barrier((notes, steer, table))
    windows = cut_windows(
        foot, notes, place, raw, rim.reshape(planes, blocks, NP, RIM), table, 4 if paired else 1
    )
    if paired:
        windows = exchange(windows)
    else:
        sent = windows[0].reshape((tiles, CAP, 2, NP, WIN))
        got = lax.all_to_all(sent, "tile", 0, 0, tiled=True)
        windows = (got.reshape(windows[0].shape),)
    return tile_image(foot, windows, steer)[None, None]


def solution(mesh):
    in_specs = (P(None, "tile", "section"), P("section", "tile", None), P("section", "tile"))
    out_specs = P("section", "tile", None, None)
    return jax.shard_map(local, mesh=mesh, in_specs=in_specs, out_specs=out_specs, check_vma=False)
```

```python
import functools
import math

import jax
import jax.numpy as jnp
import ml_dtypes
import numpy as np
from jax import lax
from jax.experimental import pallas as pl
from jax.experimental.pallas import tpu as pltpu
from jax.sharding import PartitionSpec as P

KC = 128
WIN = 256
PR = 1024
PC = 1024
NP = 8
CAP = 2
LANES = 128
PRIME = 65521
RIM = WIN + KC
TURNS = (2, 5, 7)
SPAN = RIM + LANES
ROWS = 256
BF16 = jnp.bfloat16


def vmem_grant(chunks, more=0):
    return (2 + chunks // 4 + more) << 20


def passed_along(value, axis, by):
    devices = lax.axis_size(axis)
    pairs = [(i, i + by) for i in range(devices) if 0 <= i + by < devices]
    return lax.ppermute(value, axis, pairs)


def correlation_table():
    lag = np.arange(RIM)[:, None] - np.arange(WIN)[None, :]
    inside = (lag >= 0) & (lag < KC)
    lag = np.where(inside, lag, 0)
    angle = (lag * lag % (2 * KC)).astype(np.float64) * (math.pi / KC)
    scale = 1.0 / math.sqrt(KC)
    real = np.where(inside, np.cos(angle) * scale, 0.0)
    imag = np.where(inside, np.sin(angle) * scale, 0.0)
    return np.concatenate([real, imag], axis=1).astype(np.float32).astype(ml_dtypes.bfloat16)


def interp_table():
    row = np.arange(PR, dtype=np.float64)[:, None]
    offset = np.arange(WIN, dtype=np.float64)[None, :] - ((row + 0.5) / (PR // WIN) - 0.5)
    taper = np.cos(offset * (math.pi / 8.0)) ** 2
    kernel = np.where(np.abs(offset) < 4.0, np.sinc(offset) * taper, 0.0)
    return kernel.astype(np.float32).astype(ml_dtypes.bfloat16)


def named_blocks(notes_ref, row, foot, holder, blocks):
    lowest, highest, count = jnp.int32(blocks - 1), jnp.int32(0), jnp.int32(0)
    for e in range(foot):
        block = notes_ref[row, e] - holder * blocks
        held = (block >= 0) & (block < blocks)
        lowest = jnp.where(held, jnp.minimum(lowest, block), lowest)
        highest = jnp.where(held, jnp.maximum(highest, block), highest)
        count = count + held.astype(jnp.int32)
    return lowest, highest, count


def fetch_kernel(foot, paired, notes_ref, place_ref, raw_ref, out_ref, plan_ref, sem):
    blocks = raw_ref.shape[1]
    last = (raw_ref.shape[3] - SPAN) // LANES
    mine = place_ref[1]
    own_note = mine ^ place_ref[2]

    def one_tile(n, row):
        for slot, block in enumerate(named_blocks(notes_ref, row, foot, mine, blocks)[:CAP]):
            chunk = n * CAP + slot
            start = notes_ref[own_note, foot + block]
            first = pl.multiple_of(jnp.minimum(start >> 7, last) * LANES, LANES)
            pltpu.make_async_copy(
                raw_ref.at[:, block, :, pl.ds(first, SPAN)], out_ref.at[chunk], sem
            ).start()
            plan_ref[0, chunk] = block
            plan_ref[1, chunk] = jnp.maximum((start >> 7) - last, 0)
            plan_ref[2, chunk] = lax.rem(SPAN - (start & (LANES - 1)), SPAN)

    tiles = notes_ref.shape[0]
    if paired:
        for n in range(tiles):
            one_tile(n, row_of(n, paired))
    else:
        pl.loop(0, tiles)(lambda n: one_tile(n, n))
    pltpu.make_async_copy(out_ref, out_ref, sem).wait()


def cut_kernel(plan_ref, spans_ref, rim_ref, table_ref, *refs):
    *out_refs, echo = refs
    chunks = spans_ref.shape[0]
    span_tiles = SPAN // LANES

    def one_chunk(chunk, carry):
        block, over, turn = (plan_ref[row, chunk] for row in range(3))
        pieces = []
        for step in range(span_tiles):
            own = pl.multiple_of(jnp.minimum(step + over, span_tiles - 1) * LANES, LANES)
            piece = spans_ref[chunk, :, :, pl.ds(own, LANES)].astype(jnp.float32)
            if step:
                beyond = pl.multiple_of(jnp.maximum(step + over - span_tiles, 0) * LANES, LANES)
                rim = rim_ref[:, block, :, pl.ds(beyond, LANES)].astype(jnp.float32)
                piece = jnp.where(step + over < span_tiles, piece, rim)
            pieces.append(piece)
        span = jnp.concatenate(pieces, axis=2).reshape(2 * NP, SPAN)
        rows = pl.ds(pl.multiple_of(chunk * 2 * NP, 2 * NP), 2 * NP)
        echo[rows, :] = pltpu.roll(span, turn, 1)[:, :RIM].astype(BF16)
        return carry

    lax.fori_loop(0, chunks, one_chunk, 0, unroll=chunks <= 16)
    sums = jnp.dot(echo[...], table_ref[...], preferred_element_type=jnp.float32)
    sums = sums.reshape(chunks, 2, NP, 2 * WIN)
    real = (sums[:, 0, :, :WIN] + sums[:, 1, :, WIN:]).astype(BF16)
    imag = (sums[:, 1, :, :WIN] - sums[:, 0, :, WIN:]).astype(BF16)
    each = chunks // len(out_refs)
    for group, out_ref in enumerate(out_refs):
        part = slice(group * each, (group + 1) * each)
        out_ref[:, 0] = real[part]
        out_ref[:, 1] = imag[part]


def cut_windows(foot, notes, place, raw, rim, table, groups):
    chunks = notes.shape[0] * CAP
    smem = pl.BlockSpec(memory_space=pltpu.SMEM)
    vmem = pl.BlockSpec(memory_space=pltpu.VMEM)
    params = pltpu.CompilerParams(vmem_limit_bytes=vmem_grant(chunks))
    spans, plan = pl.pallas_call(
        functools.partial(fetch_kernel, foot, groups > 1),
        out_shape=(
            jax.ShapeDtypeStruct((chunks, 2, NP, SPAN), BF16),
            jax.ShapeDtypeStruct((3, chunks), jnp.int32),
        ),
        in_specs=[smem, smem, pl.BlockSpec(memory_space=pltpu.HBM)],
        out_specs=(vmem, smem),
        scratch_shapes=[pltpu.SemaphoreType.DMA],
        compiler_params=params,
        name="fetch",
    )(notes, place, pltpu.with_memory_space_constraint(raw, pltpu.HBM))
    return pl.pallas_call(
        cut_kernel,
        out_shape=(jax.ShapeDtypeStruct((chunks // groups, 2, NP, WIN), BF16),) * groups,
        in_specs=[smem, vmem, vmem, vmem],
        out_specs=(vmem,) * groups,
        scratch_shapes=[pltpu.VMEM((chunks * 2 * NP, RIM), BF16)],
        compiler_params=params,
        name="cut",
    )(plan, spans, rim, table)


def mod_prime(value):
    for _ in range(2):
        value = (value >> 16) * 15 + (value & 65535)
    return jnp.where(value >= PRIME, value - PRIME, value)


def steer_kernel(foot, blocks, order, note_ref, place_ref, table_ref, out_ref, held_ref, sem):
    holding = pltpu.make_async_copy(table_ref, held_ref, sem)
    holding.start()
    chunks = len(order) * CAP
    to_angle = jnp.float32(2.0 * math.pi / PRIME)
    first, twist = place_ref[0], place_ref[2]

    def turned(steps, rows):
        columns = lax.broadcasted_iota(jnp.int32, (rows, PC), 1)
        scrambled = mod_prime((columns + first) * 40503)
        return mod_prime(steps * scrambled).astype(jnp.float32) * to_angle

    inner = turned(lax.broadcasted_iota(jnp.int32, (NP, PC), 0), NP)
    cos_in, sin_in = jnp.cos(inner), jnp.sin(inner)
    row = lax.broadcasted_iota(jnp.int32, (chunks, PC), 0)
    ids = jnp.zeros((chunks, PC), jnp.int32)
    used = jnp.zeros((chunks, PC), jnp.float32)
    for n, position in enumerate(order):
        holder = position ^ twist
        *found, count = named_blocks(note_ref, 0, foot, holder, blocks)
        for slot, block in enumerate(found):
            here = row == n * CAP + slot
            ids = jnp.where(here, (holder * blocks + block) * NP, ids)
            used = jnp.where(here & (count > slot), 1.0, used)
    outer = turned(ids, chunks)
    cos_out, sin_out = jnp.cos(outer) * used, jnp.sin(outer) * used
    for i in range(chunks):
        c, s = cos_out[i : i + 1], sin_out[i : i + 1]
        real = c * cos_in - s * sin_in
        imag = s * cos_in + c * sin_in
        rows = slice(i * 2 * NP, (i + 1) * 2 * NP)
        out_ref[rows, :PC] = jnp.concatenate([real, -imag], axis=0).astype(BF16)
        out_ref[rows, PC:] = jnp.concatenate([imag, real], axis=0).astype(BF16)
    holding.wait()


def steering(foot, blocks, order, note, place):
    smem = pl.BlockSpec(memory_space=pltpu.SMEM)
    vmem = pl.BlockSpec(memory_space=pltpu.VMEM)
    hbm = pl.BlockSpec(memory_space=pltpu.HBM)
    table = jnp.asarray(correlation_table())
    rows = len(order) * CAP * 2 * NP
    return pl.pallas_call(
        functools.partial(steer_kernel, foot, blocks, order),
        out_shape=(
            jax.ShapeDtypeStruct((rows, 2 * PC), BF16),
            jax.ShapeDtypeStruct(table.shape, BF16),
        ),
        in_specs=[smem, smem, hbm],
        out_specs=(vmem, vmem),
        scratch_shapes=[pltpu.SemaphoreType.DMA],
        compiler_params=pltpu.CompilerParams(vmem_limit_bytes=vmem_grant(len(order) * CAP)),
        cost_estimate=pl.CostEstimate(flops=0, bytes_accessed=4 << 20, transcendentals=0),
        name="steer",
    )(note, place, pltpu.with_memory_space_constraint(table, pltpu.HBM))


def image_kernel(scale, *refs):
    *window_refs, steer_ref, interp_ref, out_ref, focused, pixels, sem = refs
    windows = jnp.concatenate(
        [ref[...].reshape(ref.shape[0] * 2 * NP, WIN) for ref in window_refs], axis=0
    )
    contract = (((0,), (0,)), ((), ()))
    focused[...] = (
        lax.dot_general(windows, steer_ref[...], contract, preferred_element_type=jnp.float32)
        * jnp.float32(scale)
    ).astype(BF16)
    copies = []
    for step in range(PR // ROWS):
        rows = pl.ds(step * ROWS, ROWS)
        pixels[rows, :] = jnp.dot(
            interp_ref[rows, :], focused[...], preferred_element_type=jnp.float32
        ).astype(BF16)
        copy = pltpu.make_async_copy(pixels.at[rows], out_ref.at[rows], sem.at[step])
        copy.start()
        copies.append(copy)
    for copy in copies:
        copy.wait()


def tile_image(foot, windows, steer):
    vmem = pl.BlockSpec(memory_space=pltpu.VMEM)
    return pl.pallas_call(
        functools.partial(image_kernel, 1.0 / math.sqrt(foot * NP)),
        out_shape=jax.ShapeDtypeStruct((PR, 2 * PC), BF16),
        in_specs=[vmem] * (len(windows) + 2),
        out_specs=pl.BlockSpec(memory_space=pltpu.HBM),
        scratch_shapes=[
            pltpu.VMEM((WIN, 2 * PC), BF16),
            pltpu.VMEM((PR, 2 * PC), BF16),
            pltpu.SemaphoreType.DMA((PR // ROWS,)),
        ],
        compiler_params=pltpu.CompilerParams(vmem_limit_bytes=vmem_grant(steer.shape[0] // (2 * NP), 5)),
        name="image",
    )(*windows, steer, jnp.asarray(interp_table()))


def swapped(value, turn):
    tiles = lax.axis_size("tile")
    return lax.ppermute(value, "tile", [(i, i ^ turn) for i in range(tiles)])


def gather_notes(note):
    pair = jnp.concatenate([note, swapped(note, 1)], axis=0)
    return jnp.concatenate([pair] + [swapped(pair, turn) for turn in TURNS], axis=0)


def row_of(position, paired):
    turns = (0,) + TURNS
    if not paired:
        return position
    return 2 * (position // 2) + (position ^ turns[position // 2]) % 2


def exchange(windows):
    ours, theirs = [windows[0][:CAP]], [windows[0][CAP:]]
    for window, turn in zip(windows[1:], TURNS):
        got = swapped(window, turn)
        halves = (got[:CAP], got[CAP:])
        ours.append(halves[turn % 2])
        theirs.append(halves[1 - turn % 2])
    return jnp.concatenate(ours, axis=0), swapped(jnp.concatenate(theirs, axis=0), 1)


def local(raw_echo, footprint, window_start):
    planes, pulses, bins = raw_echo.shape
    blocks = pulses // NP
    tiles = lax.axis_size("tile")
    paired = tiles == 8
    foot = footprint.shape[2]
    tile_pos = lax.axis_index("tile").astype(jnp.int32)
    row_pos = lax.axis_index("section").astype(jnp.int32)

    rim = passed_along(raw_echo[:, :, :RIM], "section", -1)
    note = jnp.concatenate([footprint[0], window_start], axis=1)
    note = jnp.pad(note, ((0, 0), (0, -note.shape[1] % LANES)))
    notes = gather_notes(note) if paired else lax.all_gather(note, "tile", axis=0, tiled=True)
    twist = tile_pos if paired else jnp.int32(0)
    place = jnp.stack([tile_pos * PC + 1 + 7 * row_pos, tile_pos, twist])
    order = tuple(range(tiles))
    if paired:
        order = (0,) + TURNS + (1,) + tuple(turn ^ 1 for turn in TURNS)

    raw = raw_echo.reshape(planes, blocks, NP, bins)
    steer, table = steering(foot, blocks, order, note, place)
    notes, steer, table = lax.optimization_barrier((notes, steer, table))
    windows = cut_windows(
        foot, notes, place, raw, rim.reshape(planes, blocks, NP, RIM), table, 4 if paired else 1
    )
    if paired:
        windows = exchange(windows)
    else:
        sent = windows[0].reshape((tiles, CAP, 2, NP, WIN))
        got = lax.all_to_all(sent, "tile", 0, 0, tiled=True)
        windows = (got.reshape(windows[0].shape),)
    return tile_image(foot, windows, steer)[None, None]


def solution(mesh):
    in_specs = (P(None, "tile", "section"), P("section", "tile", None), P("section", "tile"))
    out_specs = P("section", "tile", None, None)
    return jax.shard_map(local, mesh=mesh, in_specs=in_specs, out_specs=out_specs, check_vma=False)
```

```python
import functools
import math

import jax
import jax.numpy as jnp
import ml_dtypes
import numpy as np
from jax import lax
from jax.experimental import pallas as pl
from jax.experimental.pallas import tpu as pltpu
from jax.sharding import PartitionSpec as P

KC = 128
WIN = 256
PR = 1024
PC = 1024
NP = 8
CAP = 2
LANES = 128
PRIME = 65521
RIM = WIN + KC
TURNS = (2, 5, 7)
SPAN = RIM + LANES
ROWS = 256
BF16 = jnp.bfloat16


def vmem_grant(chunks, more=0):
    return (2 + chunks // 4 + more) << 20


def passed_along(value, axis, by):
    devices = lax.axis_size(axis)
    pairs = [(i, i + by) for i in range(devices) if 0 <= i + by < devices]
    return lax.ppermute(value, axis, pairs)


def correlation_table():
    lag = np.arange(RIM)[:, None] - np.arange(WIN)[None, :]
    inside = (lag >= 0) & (lag < KC)
    lag = np.where(inside, lag, 0)
    angle = (lag * lag % (2 * KC)).astype(np.float64) * (math.pi / KC)
    scale = 1.0 / math.sqrt(KC)
    real = np.where(inside, np.cos(angle) * scale, 0.0)
    imag = np.where(inside, np.sin(angle) * scale, 0.0)
    return np.concatenate([real, imag], axis=1).astype(np.float32).astype(ml_dtypes.bfloat16)


def interp_table():
    row = np.arange(PR, dtype=np.float64)[:, None]
    offset = np.arange(WIN, dtype=np.float64)[None, :] - ((row + 0.5) / (PR // WIN) - 0.5)
    taper = np.cos(offset * (math.pi / 8.0)) ** 2
    kernel = np.where(np.abs(offset) < 4.0, np.sinc(offset) * taper, 0.0)
    return kernel.astype(np.float32).astype(ml_dtypes.bfloat16)


def named_blocks(notes_ref, row, foot, holder, blocks):
    lowest, highest, count = jnp.int32(blocks - 1), jnp.int32(0), jnp.int32(0)
    for e in range(foot):
        block = notes_ref[row, e] - holder * blocks
        held = (block >= 0) & (block < blocks)
        lowest = jnp.where(held, jnp.minimum(lowest, block), lowest)
        highest = jnp.where(held, jnp.maximum(highest, block), highest)
        count = count + held.astype(jnp.int32)
    return lowest, highest, count


def plan_of(foot, blocks, last, mine, note, notes):
    lane = lax.broadcasted_iota(jnp.int32, notes.shape, 1)
    block = notes - mine * blocks
    held = (lane < foot) & (block >= 0) & (block < blocks)
    block = block.astype(jnp.float32)
    lowest = jnp.min(jnp.where(held, block, blocks - 1.0), axis=1, keepdims=True)
    highest = jnp.max(jnp.where(held, block, 0.0), axis=1, keepdims=True)
    starts = jnp.broadcast_to(note, notes.shape).astype(jnp.float32)
    plan = jnp.zeros(notes.shape, jnp.int32)
    for slot, block in enumerate((lowest, highest)):
        block = block.astype(jnp.int32)
        start = jnp.sum(jnp.where(lane == foot + block, starts, 0.0), axis=1, keepdims=True)
        start = start.astype(jnp.int32)
        tile = start >> 7
        turn = (SPAN - (start & (LANES - 1))) & (SPAN - 1)
        code = (block * 4 + jnp.maximum(tile - last, 0)) * 64 + jnp.minimum(tile, last)
        plan = jnp.where(lane == slot, code * SPAN + turn, plan)
    return plan


def planned(code):
    return code >> 17, (code >> 15) & 3, (code >> 9) & 63, code & (SPAN - 1)


def chunk_places(tiles, paired):
    return [(row_of(n, paired), slot) for n in range(tiles) for slot in range(CAP)]


def fetch_kernel(foot, paired, place_ref, note_ref, notes_ref, raw_ref, out_ref, plan_ref, sem):
    blocks = raw_ref.shape[1]
    last = (raw_ref.shape[3] - SPAN) // LANES
    plan = plan_of(foot, blocks, last, place_ref[0:1, 1:2], note_ref[...], notes_ref[...])
    for chunk, (row, slot) in enumerate(chunk_places(notes_ref.shape[0], paired)):
        block, _, first, _ = planned(plan[row, slot])
        lanes = pl.ds(pl.multiple_of(first * LANES, LANES), SPAN)
        pltpu.make_async_copy(raw_ref.at[:, block, :, lanes], out_ref.at[chunk], sem).start()
    plan_ref[...] = plan
    pltpu.make_async_copy(out_ref, out_ref, sem).wait()


def cut_kernel(paired, plan_ref, spans_ref, rim_ref, table_ref, *refs):
    *out_refs, echo = refs
    chunks = spans_ref.shape[0]
    span_tiles = SPAN // LANES
    plan = plan_ref[...]
    for chunk, (row, slot) in enumerate(chunk_places(chunks // CAP, paired)):
        block, over, _, turn = planned(plan[row, slot])
        pieces = []
        for step in range(span_tiles):
            own = pl.multiple_of(jnp.minimum(step + over, span_tiles - 1) * LANES, LANES)
            piece = spans_ref[chunk, :, :, pl.ds(own, LANES)].astype(jnp.float32)
            if step:
                beyond = pl.multiple_of(jnp.maximum(step + over - span_tiles, 0) * LANES, LANES)
                rim = rim_ref[:, block, :, pl.ds(beyond, LANES)].astype(jnp.float32)
                piece = jnp.where(step + over < span_tiles, piece, rim)
            pieces.append(piece)
        span = jnp.concatenate(pieces, axis=2).reshape(2 * NP, SPAN)
        rows = slice(chunk * 2 * NP, (chunk + 1) * 2 * NP)
        echo[rows, :] = pltpu.roll(span, turn, 1)[:, :RIM].astype(BF16)
    sums = jnp.dot(echo[...], table_ref[...], preferred_element_type=jnp.float32)
    sums = sums.reshape(chunks, 2, NP, 2 * WIN)
    real = (sums[:, 0, :, :WIN] + sums[:, 1, :, WIN:]).astype(BF16)
    imag = (sums[:, 1, :, :WIN] - sums[:, 0, :, WIN:]).astype(BF16)
    each = chunks // len(out_refs)
    for group, out_ref in enumerate(out_refs):
        part = slice(group * each, (group + 1) * each)
        out_ref[:, 0] = real[part]
        out_ref[:, 1] = imag[part]


def cut_windows(foot, note, notes, place, raw, rim, table, groups):
    chunks = notes.shape[0] * CAP
    vmem = pl.BlockSpec(memory_space=pltpu.VMEM)
    params = pltpu.CompilerParams(vmem_limit_bytes=vmem_grant(chunks))
    spans, plan = pl.pallas_call(
        functools.partial(fetch_kernel, foot, groups > 1),
        out_shape=(
            jax.ShapeDtypeStruct((chunks, 2, NP, SPAN), BF16),
            jax.ShapeDtypeStruct(notes.shape, jnp.int32),
        ),
        in_specs=[vmem, vmem, vmem, pl.BlockSpec(memory_space=pltpu.HBM)],
        out_specs=(vmem, vmem),
        scratch_shapes=[pltpu.SemaphoreType.DMA],
        compiler_params=params,
        name="fetch",
    )(place[None], note, notes, pltpu.with_memory_space_constraint(raw, pltpu.HBM))
    return pl.pallas_call(
        functools.partial(cut_kernel, groups > 1),
        out_shape=(jax.ShapeDtypeStruct((chunks // groups, 2, NP, WIN), BF16),) * groups,
        in_specs=[vmem] * 4,
        out_specs=(vmem,) * groups,
        scratch_shapes=[pltpu.VMEM((chunks * 2 * NP, RIM), BF16)],
        compiler_params=params,
        name="cut",
    )(plan, spans, rim, table)


def mod_prime(value):
    for _ in range(2):
        value = (value >> 16) * 15 + (value & 65535)
    return jnp.where(value >= PRIME, value - PRIME, value)


def steer_kernel(foot, blocks, order, note_ref, place_ref, table_ref, out_ref, held_ref, sem):
    holding = pltpu.make_async_copy(table_ref, held_ref, sem)
    holding.start()
    chunks = len(order) * CAP
    to_angle = jnp.float32(2.0 * math.pi / PRIME)
    first, twist = place_ref[0], place_ref[2]

    def turned(steps, rows):
        columns = lax.broadcasted_iota(jnp.int32, (rows, PC), 1)
        scrambled = mod_prime((columns + first) * 40503)
        return mod_prime(steps * scrambled).astype(jnp.float32) * to_angle

    inner = turned(lax.broadcasted_iota(jnp.int32, (NP, PC), 0), NP)
    cos_in, sin_in = jnp.cos(inner), jnp.sin(inner)
    row = lax.broadcasted_iota(jnp.int32, (chunks, PC), 0)
    ids = jnp.zeros((chunks, PC), jnp.int32)
    used = jnp.zeros((chunks, PC), jnp.float32)
    for n, position in enumerate(order):
        holder = position ^ twist
        *found, count = named_blocks(note_ref, 0, foot, holder, blocks)
        for slot, block in enumerate(found):
            here = row == n * CAP + slot
            ids = jnp.where(here, (holder * blocks + block) * NP, ids)
            used = jnp.where(here & (count > slot), 1.0, used)
    outer = turned(ids, chunks)
    cos_out, sin_out = jnp.cos(outer) * used, jnp.sin(outer) * used
    for i in range(chunks):
        c, s = cos_out[i : i + 1], sin_out[i : i + 1]
        real = c * cos_in - s * sin_in
        imag = s * cos_in + c * sin_in
        rows = slice(i * 2 * NP, (i + 1) * 2 * NP)
        out_ref[rows, :PC] = jnp.concatenate([real, -imag], axis=0).astype(BF16)
        out_ref[rows, PC:] = jnp.concatenate([imag, real], axis=0).astype(BF16)
    holding.wait()


def steering(foot, blocks, order, note, place):
    smem = pl.BlockSpec(memory_space=pltpu.SMEM)
    vmem = pl.BlockSpec(memory_space=pltpu.VMEM)
    hbm = pl.BlockSpec(memory_space=pltpu.HBM)
    table = jnp.asarray(correlation_table())
    rows = len(order) * CAP * 2 * NP
    return pl.pallas_call(
        functools.partial(steer_kernel, foot, blocks, order),
        out_shape=(
            jax.ShapeDtypeStruct((rows, 2 * PC), BF16),
            jax.ShapeDtypeStruct(table.shape, BF16),
        ),
        in_specs=[smem, smem, hbm],
        out_specs=(vmem, vmem),
        scratch_shapes=[pltpu.SemaphoreType.DMA],
        compiler_params=pltpu.CompilerParams(vmem_limit_bytes=vmem_grant(len(order) * CAP)),
        cost_estimate=pl.CostEstimate(flops=0, bytes_accessed=4 << 20, transcendentals=0),
        name="steer",
    )(note, place, pltpu.with_memory_space_constraint(table, pltpu.HBM))


def image_kernel(scale, *refs):
    *window_refs, steer_ref, interp_ref, out_ref, focused, pixels, sem = refs
    windows = jnp.concatenate(
        [ref[...].reshape(ref.shape[0] * 2 * NP, WIN) for ref in window_refs], axis=0
    )
    contract = (((0,), (0,)), ((), ()))
    focused[...] = (
        lax.dot_general(windows, steer_ref[...], contract, preferred_element_type=jnp.float32)
        * jnp.float32(scale)
    ).astype(BF16)
    copies = []
    for step in range(PR // ROWS):
        rows = pl.ds(step * ROWS, ROWS)
        pixels[rows, :] = jnp.dot(
            interp_ref[rows, :], focused[...], preferred_element_type=jnp.float32
        ).astype(BF16)
        copy = pltpu.make_async_copy(pixels.at[rows], out_ref.at[rows], sem.at[step])
        copy.start()
        copies.append(copy)
    for copy in copies:
        copy.wait()


def tile_image(foot, windows, steer):
    vmem = pl.BlockSpec(memory_space=pltpu.VMEM)
    return pl.pallas_call(
        functools.partial(image_kernel, 1.0 / math.sqrt(foot * NP)),
        out_shape=jax.ShapeDtypeStruct((PR, 2 * PC), BF16),
        in_specs=[vmem] * (len(windows) + 2),
        out_specs=pl.BlockSpec(memory_space=pltpu.HBM),
        scratch_shapes=[
            pltpu.VMEM((WIN, 2 * PC), BF16),
            pltpu.VMEM((PR, 2 * PC), BF16),
            pltpu.SemaphoreType.DMA((PR // ROWS,)),
        ],
        compiler_params=pltpu.CompilerParams(vmem_limit_bytes=vmem_grant(steer.shape[0] // (2 * NP), 5)),
        name="image",
    )(*windows, steer, jnp.asarray(interp_table()))


def swapped(value, turn):
    tiles = lax.axis_size("tile")
    return lax.ppermute(value, "tile", [(i, i ^ turn) for i in range(tiles)])


def gather_notes(note):
    pair = jnp.concatenate([note, swapped(note, 1)], axis=0)
    return jnp.concatenate([pair] + [swapped(pair, turn) for turn in TURNS], axis=0)


def row_of(position, paired):
    turns = (0,) + TURNS
    if not paired:
        return position
    return 2 * (position // 2) + (position ^ turns[position // 2]) % 2


def exchange(windows):
    ours, theirs = [windows[0][:CAP]], [windows[0][CAP:]]
    for window, turn in zip(windows[1:], TURNS):
        got = swapped(window, turn)
        halves = (got[:CAP], got[CAP:])
        ours.append(halves[turn % 2])
        theirs.append(halves[1 - turn % 2])
    return jnp.concatenate(ours, axis=0), swapped(jnp.concatenate(theirs, axis=0), 1)


def local(raw_echo, footprint, window_start):
    planes, pulses, bins = raw_echo.shape
    blocks = pulses // NP
    tiles = lax.axis_size("tile")
    paired = tiles == 8
    foot = footprint.shape[2]
    tile_pos = lax.axis_index("tile").astype(jnp.int32)
    row_pos = lax.axis_index("section").astype(jnp.int32)

    rim = passed_along(raw_echo[:, :, :RIM], "section", -1)
    note = jnp.concatenate([footprint[0], window_start], axis=1)
    note = jnp.pad(note, ((0, 0), (0, -note.shape[1] % LANES)))
    notes = gather_notes(note) if paired else lax.all_gather(note, "tile", axis=0, tiled=True)
    twist = tile_pos if paired else jnp.int32(0)
    place = jnp.stack([tile_pos * PC + 1 + 7 * row_pos, tile_pos, twist])
    order = tuple(range(tiles))
    if paired:
        order = (0,) + TURNS + (1,) + tuple(turn ^ 1 for turn in TURNS)

    raw = raw_echo.reshape(planes, blocks, NP, bins)
    steer, table = steering(foot, blocks, order, note, place)
    notes, steer, table = lax.optimization_barrier((notes, steer, table))
    windows = cut_windows(
        foot, note, notes, place, raw, rim.reshape(planes, blocks, NP, RIM), table, 4 if paired else 1
    )
    if paired:
        windows = exchange(windows)
    else:
        sent = windows[0].reshape((tiles, CAP, 2, NP, WIN))
        got = lax.all_to_all(sent, "tile", 0, 0, tiled=True)
        windows = (got.reshape(windows[0].shape),)
    return tile_image(foot, windows, steer)[None, None]


def solution(mesh):
    in_specs = (P(None, "tile", "section"), P("section", "tile", None), P("section", "tile"))
    out_specs = P("section", "tile", None, None)
    return jax.shard_map(local, mesh=mesh, in_specs=in_specs, out_specs=out_specs, check_vma=False)
```

```python
import functools
import math

import jax
import jax.numpy as jnp
import ml_dtypes
import numpy as np
from jax import lax
from jax.experimental import pallas as pl
from jax.experimental.pallas import tpu as pltpu
from jax.sharding import PartitionSpec as P

KC = 128
WIN = 256
PR = 1024
PC = 1024
NP = 8
CAP = 2
LANES = 128
PRIME = 65521
RIM = WIN + KC
TURNS = (2, 5, 6)
SPAN = RIM + LANES
ROWS = 256
BF16 = jnp.bfloat16


def vmem_grant(chunks, more=0):
    return (2 + chunks // 4 + more) << 20


def passed_along(value, axis, by):
    devices = lax.axis_size(axis)
    pairs = [(i, i + by) for i in range(devices) if 0 <= i + by < devices]
    return lax.ppermute(value, axis, pairs)


def correlation_table():
    lag = np.arange(RIM)[:, None] - np.arange(WIN)[None, :]
    inside = (lag >= 0) & (lag < KC)
    lag = np.where(inside, lag, 0)
    angle = (lag * lag % (2 * KC)).astype(np.float64) * (math.pi / KC)
    scale = 1.0 / math.sqrt(KC)
    real = np.where(inside, np.cos(angle) * scale, 0.0)
    imag = np.where(inside, np.sin(angle) * scale, 0.0)
    return np.concatenate([real, imag], axis=1).astype(np.float32).astype(ml_dtypes.bfloat16)


def interp_table():
    row = np.arange(PR, dtype=np.float64)[:, None]
    offset = np.arange(WIN, dtype=np.float64)[None, :] - ((row + 0.5) / (PR // WIN) - 0.5)
    taper = np.cos(offset * (math.pi / 8.0)) ** 2
    kernel = np.where(np.abs(offset) < 4.0, np.sinc(offset) * taper, 0.0)
    return kernel.astype(np.float32).astype(ml_dtypes.bfloat16)


def named_blocks(notes_ref, row, foot, holder, blocks):
    lowest, highest, count = jnp.int32(blocks - 1), jnp.int32(0), jnp.int32(0)
    for e in range(foot):
        block = notes_ref[row, e] - holder * blocks
        held = (block >= 0) & (block < blocks)
        lowest = jnp.where(held, jnp.minimum(lowest, block), lowest)
        highest = jnp.where(held, jnp.maximum(highest, block), highest)
        count = count + held.astype(jnp.int32)
    return lowest, highest, count


def plan_of(foot, blocks, last, mine, note, notes):
    lane = lax.broadcasted_iota(jnp.int32, notes.shape, 1)
    block = notes - mine * blocks
    held = (lane < foot) & (block >= 0) & (block < blocks)
    block = block.astype(jnp.float32)
    lowest = jnp.min(jnp.where(held, block, blocks - 1.0), axis=1, keepdims=True)
    highest = jnp.max(jnp.where(held, block, 0.0), axis=1, keepdims=True)
    starts = jnp.broadcast_to(note, notes.shape).astype(jnp.float32)
    plan = jnp.zeros(notes.shape, jnp.int32)
    for slot, block in enumerate((lowest, highest)):
        block = block.astype(jnp.int32)
        start = jnp.sum(jnp.where(lane == foot + block, starts, 0.0), axis=1, keepdims=True)
        start = start.astype(jnp.int32)
        tile = start >> 7
        turn = (SPAN - (start & (LANES - 1))) & (SPAN - 1)
        code = (block * 4 + jnp.maximum(tile - last, 0)) * 64 + jnp.minimum(tile, last)
        plan = jnp.where(lane == slot, code * SPAN + turn, plan)
    return plan


def planned(code):
    return code >> 17, (code >> 15) & 3, (code >> 9) & 63, code & (SPAN - 1)


def chunk_places(tiles, paired):
    return [(row_of(n, paired), slot) for n in range(tiles) for slot in range(CAP)]


def fetch_kernel(foot, paired, place_ref, note_ref, notes_ref, raw_ref, out_ref, plan_ref, sem):
    blocks = raw_ref.shape[1]
    last = (raw_ref.shape[3] - SPAN) // LANES
    plan = plan_of(foot, blocks, last, place_ref[0:1, 1:2], note_ref[...], notes_ref[...])
    for chunk, (row, slot) in enumerate(chunk_places(notes_ref.shape[0], paired)):
        block, _, first, _ = planned(plan[row, slot])
        lanes = pl.ds(pl.multiple_of(first * LANES, LANES), SPAN)
        pltpu.make_async_copy(raw_ref.at[:, block, :, lanes], out_ref.at[chunk], sem).start()
    plan_ref[...] = plan
    pltpu.make_async_copy(out_ref, out_ref, sem).wait()


def cut_kernel(paired, plan_ref, spans_ref, rim_ref, table_ref, *refs):
    *out_refs, echo = refs
    chunks = spans_ref.shape[0]
    span_tiles = SPAN // LANES
    plan = plan_ref[...]
    for chunk, (row, slot) in enumerate(chunk_places(chunks // CAP, paired)):
        block, over, _, turn = planned(plan[row, slot])
        pieces = []
        for step in range(span_tiles):
            own = pl.multiple_of(jnp.minimum(step + over, span_tiles - 1) * LANES, LANES)
            piece = spans_ref[chunk, :, :, pl.ds(own, LANES)].astype(jnp.float32)
            if step:
                beyond = pl.multiple_of(jnp.maximum(step + over - span_tiles, 0) * LANES, LANES)
                rim = rim_ref[:, block, :, pl.ds(beyond, LANES)].astype(jnp.float32)
                piece = jnp.where(step + over < span_tiles, piece, rim)
            pieces.append(piece)
        span = jnp.concatenate(pieces, axis=2).reshape(2 * NP, SPAN)
        rows = slice(chunk * 2 * NP, (chunk + 1) * 2 * NP)
        echo[rows, :] = pltpu.roll(span, turn, 1)[:, :RIM].astype(BF16)
    sums = jnp.dot(echo[...], table_ref[...], preferred_element_type=jnp.float32)
    sums = sums.reshape(chunks, 2, NP, 2 * WIN)
    real = (sums[:, 0, :, :WIN] + sums[:, 1, :, WIN:]).astype(BF16)
    imag = (sums[:, 1, :, :WIN] - sums[:, 0, :, WIN:]).astype(BF16)
    each = chunks // len(out_refs)
    for group, out_ref in enumerate(out_refs):
        part = slice(group * each, (group + 1) * each)
        out_ref[:, 0] = real[part]
        out_ref[:, 1] = imag[part]


def cut_windows(foot, note, notes, place, raw, rim, table, groups):
    chunks = notes.shape[0] * CAP
    vmem = pl.BlockSpec(memory_space=pltpu.VMEM)
    params = pltpu.CompilerParams(vmem_limit_bytes=vmem_grant(chunks))
    spans, plan = pl.pallas_call(
        functools.partial(fetch_kernel, foot, groups > 1),
        out_shape=(
            jax.ShapeDtypeStruct((chunks, 2, NP, SPAN), BF16),
            jax.ShapeDtypeStruct(notes.shape, jnp.int32),
        ),
        in_specs=[vmem, vmem, vmem, pl.BlockSpec(memory_space=pltpu.HBM)],
        out_specs=(vmem, vmem),
        scratch_shapes=[pltpu.SemaphoreType.DMA],
        compiler_params=params,
        name="fetch",
    )(place[None], note, notes, pltpu.with_memory_space_constraint(raw, pltpu.HBM))
    return pl.pallas_call(
        functools.partial(cut_kernel, groups > 1),
        out_shape=(jax.ShapeDtypeStruct((chunks // groups, 2, NP, WIN), BF16),) * groups,
        in_specs=[vmem] * 4,
        out_specs=(vmem,) * groups,
        scratch_shapes=[pltpu.VMEM((chunks * 2 * NP, RIM), BF16)],
        compiler_params=params,
        name="cut",
    )(plan, spans, rim, table)


def mod_prime(value):
    for _ in range(2):
        value = (value >> 16) * 15 + (value & 65535)
    return jnp.where(value >= PRIME, value - PRIME, value)


def steer_kernel(foot, blocks, order, note_ref, place_ref, table_ref, out_ref, held_ref, sem):
    holding = pltpu.make_async_copy(table_ref, held_ref, sem)
    holding.start()
    chunks = len(order) * CAP
    to_angle = jnp.float32(2.0 * math.pi / PRIME)
    first, twist = place_ref[0], place_ref[2]

    def turned(steps, rows):
        columns = lax.broadcasted_iota(jnp.int32, (rows, PC), 1)
        scrambled = mod_prime((columns + first) * 40503)
        return mod_prime(steps * scrambled).astype(jnp.float32) * to_angle

    inner = turned(lax.broadcasted_iota(jnp.int32, (NP, PC), 0), NP)
    cos_in, sin_in = jnp.cos(inner), jnp.sin(inner)
    row = lax.broadcasted_iota(jnp.int32, (chunks, PC), 0)
    ids = jnp.zeros((chunks, PC), jnp.int32)
    used = jnp.zeros((chunks, PC), jnp.float32)
    for n, position in enumerate(order):
        holder = position ^ twist
        *found, count = named_blocks(note_ref, 0, foot, holder, blocks)
        for slot, block in enumerate(found):
            here = row == n * CAP + slot
            ids = jnp.where(here, (holder * blocks + block) * NP, ids)
            used = jnp.where(here & (count > slot), 1.0, used)
    outer = turned(ids, chunks)
    cos_out, sin_out = jnp.cos(outer) * used, jnp.sin(outer) * used
    for i in range(chunks):
        c, s = cos_out[i : i + 1], sin_out[i : i + 1]
        real = c * cos_in - s * sin_in
        imag = s * cos_in + c * sin_in
        rows = slice(i * 2 * NP, (i + 1) * 2 * NP)
        out_ref[rows, :PC] = jnp.concatenate([real, -imag], axis=0).astype(BF16)
        out_ref[rows, PC:] = jnp.concatenate([imag, real], axis=0).astype(BF16)
    holding.wait()


def steering(foot, blocks, order, note, place):
    smem = pl.BlockSpec(memory_space=pltpu.SMEM)
    vmem = pl.BlockSpec(memory_space=pltpu.VMEM)
    hbm = pl.BlockSpec(memory_space=pltpu.HBM)
    table = jnp.asarray(correlation_table())
    rows = len(order) * CAP * 2 * NP
    return pl.pallas_call(
        functools.partial(steer_kernel, foot, blocks, order),
        out_shape=(
            jax.ShapeDtypeStruct((rows, 2 * PC), BF16),
            jax.ShapeDtypeStruct(table.shape, BF16),
        ),
        in_specs=[smem, smem, hbm],
        out_specs=(vmem, vmem),
        scratch_shapes=[pltpu.SemaphoreType.DMA],
        compiler_params=pltpu.CompilerParams(vmem_limit_bytes=vmem_grant(len(order) * CAP)),
        cost_estimate=pl.CostEstimate(flops=0, bytes_accessed=4 << 20, transcendentals=0),
        name="steer",
    )(note, place, pltpu.with_memory_space_constraint(table, pltpu.HBM))


def image_kernel(scale, *refs):
    *window_refs, steer_ref, interp_ref, out_ref, focused, pixels, sem = refs
    windows = jnp.concatenate(
        [ref[...].reshape(ref.shape[0] * 2 * NP, WIN) for ref in window_refs], axis=0
    )
    contract = (((0,), (0,)), ((), ()))
    copies = []
    for columns in (slice(0, PC), slice(PC, 2 * PC)):
        focused[:, columns] = (
            lax.dot_general(
                windows, steer_ref[:, columns], contract, preferred_element_type=jnp.float32
            )
            * jnp.float32(scale)
        ).astype(BF16)
        for first in range(0, PR, ROWS):
            part = (slice(first, first + ROWS), columns)
            pixels[part] = jnp.dot(
                interp_ref[part[0], :], focused[:, columns], preferred_element_type=jnp.float32
            ).astype(BF16)
            copy = pltpu.make_async_copy(pixels.at[part], out_ref.at[part], sem.at[len(copies)])
            copy.start()
            copies.append(copy)
    for copy in copies:
        copy.wait()


def tile_image(foot, windows, steer):
    vmem = pl.BlockSpec(memory_space=pltpu.VMEM)
    return pl.pallas_call(
        functools.partial(image_kernel, 1.0 / math.sqrt(foot * NP)),
        out_shape=jax.ShapeDtypeStruct((PR, 2 * PC), BF16),
        in_specs=[vmem] * (len(windows) + 2),
        out_specs=pl.BlockSpec(memory_space=pltpu.HBM),
        scratch_shapes=[
            pltpu.VMEM((WIN, 2 * PC), BF16),
            pltpu.VMEM((PR, 2 * PC), BF16),
            pltpu.SemaphoreType.DMA((2 * PR // ROWS,)),
        ],
        compiler_params=pltpu.CompilerParams(vmem_limit_bytes=vmem_grant(steer.shape[0] // (2 * NP), 5)),
        name="image",
    )(*windows, steer, jnp.asarray(interp_table()))


def swapped(value, turn):
    tiles = lax.axis_size("tile")
    return lax.ppermute(value, "tile", [(i, i ^ turn) for i in range(tiles)])


def gather_notes(note):
    pair = jnp.concatenate([note, swapped(note, 1)], axis=0)
    return jnp.concatenate([pair] + [swapped(pair, turn) for turn in TURNS], axis=0)


def row_of(position, paired):
    turns = (0,) + TURNS
    if not paired:
        return position
    return 2 * (position // 2) + (position ^ turns[position // 2]) % 2


def exchange(windows):
    ours, theirs = [windows[0][:CAP]], [windows[0][CAP:]]
    for window, turn in zip(windows[1:], TURNS):
        got = swapped(window, turn)
        halves = (got[:CAP], got[CAP:])
        ours.append(halves[turn % 2])
        theirs.append(halves[1 - turn % 2])
    return jnp.concatenate(ours, axis=0), swapped(jnp.concatenate(theirs, axis=0), 1)


def local(raw_echo, footprint, window_start):
    planes, pulses, bins = raw_echo.shape
    blocks = pulses // NP
    tiles = lax.axis_size("tile")
    paired = tiles == 8
    foot = footprint.shape[2]
    tile_pos = lax.axis_index("tile").astype(jnp.int32)
    row_pos = lax.axis_index("section").astype(jnp.int32)

    rim = passed_along(raw_echo[:, :, :RIM], "section", -1)
    note = jnp.concatenate([footprint[0], window_start], axis=1)
    note = jnp.pad(note, ((0, 0), (0, -note.shape[1] % LANES)))
    notes = gather_notes(note) if paired else lax.all_gather(note, "tile", axis=0, tiled=True)
    twist = tile_pos if paired else jnp.int32(0)
    place = jnp.stack([tile_pos * PC + 1 + 7 * row_pos, tile_pos, twist])
    order = tuple(range(tiles))
    if paired:
        order = (0,) + TURNS + (1,) + tuple(turn ^ 1 for turn in TURNS)

    raw = raw_echo.reshape(planes, blocks, NP, bins)
    steer, table = steering(foot, blocks, order, note, place)
    notes, steer, table = lax.optimization_barrier((notes, steer, table))
    windows = cut_windows(
        foot, note, notes, place, raw, rim.reshape(planes, blocks, NP, RIM), table, 4 if paired else 1
    )
    if paired:
        windows = exchange(windows)
    else:
        sent = windows[0].reshape((tiles, CAP, 2, NP, WIN))
        got = lax.all_to_all(sent, "tile", 0, 0, tiled=True)
        windows = (got.reshape(windows[0].shape),)
    return tile_image(foot, windows, steer)[None, None]


def solution(mesh):
    in_specs = (P(None, "tile", "section"), P("section", "tile", None), P("section", "tile"))
    out_specs = P("section", "tile", None, None)
    return jax.shard_map(local, mesh=mesh, in_specs=in_specs, out_specs=out_specs, check_vma=False)
```

```python
import functools
import math

import jax
import jax.numpy as jnp
import ml_dtypes
import numpy as np
from jax import lax
from jax.experimental import pallas as pl
from jax.experimental.pallas import tpu as pltpu
from jax.sharding import PartitionSpec as P

KC = 128
WIN = 256
PR = 1024
PC = 1024
NP = 8
CAP = 2
LANES = 128
PRIME = 65521
RIM = WIN + KC
TURNS = (2, 5, 6)
SPAN = RIM + LANES
ROWS = 256
BF16 = jnp.bfloat16


def vmem_grant(chunks, more=0):
    return (2 + chunks // 4 + more) << 20


def passed_along(value, axis, by):
    devices = lax.axis_size(axis)
    pairs = [(i, i + by) for i in range(devices) if 0 <= i + by < devices]
    return lax.ppermute(value, axis, pairs)


def correlation_table():
    lag = np.arange(2 * KC)[:, None] - np.arange(KC)[None, :]
    inside = (lag >= 0) & (lag < KC)
    lag = np.where(inside, lag, 0)
    angle = (lag * lag % (2 * KC)).astype(np.float64) * (math.pi / KC)
    scale = 1.0 / math.sqrt(KC)
    real = np.where(inside, np.cos(angle) * scale, 0.0)
    imag = np.where(inside, np.sin(angle) * scale, 0.0)
    return np.concatenate([real, imag], axis=1).astype(np.float32).astype(ml_dtypes.bfloat16)


def interp_table():
    row = np.arange(PR, dtype=np.float64)[:, None]
    offset = np.arange(WIN, dtype=np.float64)[None, :] - ((row + 0.5) / (PR // WIN) - 0.5)
    taper = np.cos(offset * (math.pi / 8.0)) ** 2
    kernel = np.where(np.abs(offset) < 4.0, np.sinc(offset) * taper, 0.0)
    return kernel.astype(np.float32).astype(ml_dtypes.bfloat16)


def named_blocks(notes_ref, row, foot, holder, blocks):
    lowest, highest, count = jnp.int32(blocks - 1), jnp.int32(0), jnp.int32(0)
    for e in range(foot):
        block = notes_ref[row, e] - holder * blocks
        held = (block >= 0) & (block < blocks)
        lowest = jnp.where(held, jnp.minimum(lowest, block), lowest)
        highest = jnp.where(held, jnp.maximum(highest, block), highest)
        count = count + held.astype(jnp.int32)
    return lowest, highest, count


def plan_of(foot, blocks, last, mine, note, notes):
    lane = lax.broadcasted_iota(jnp.int32, notes.shape, 1)
    block = notes - mine * blocks
    held = (lane < foot) & (block >= 0) & (block < blocks)
    block = block.astype(jnp.float32)
    lowest = jnp.min(jnp.where(held, block, blocks - 1.0), axis=1, keepdims=True)
    highest = jnp.max(jnp.where(held, block, 0.0), axis=1, keepdims=True)
    starts = jnp.broadcast_to(note, notes.shape).astype(jnp.float32)
    plan = jnp.zeros(notes.shape, jnp.int32)
    for slot, block in enumerate((lowest, highest)):
        block = block.astype(jnp.int32)
        start = jnp.sum(jnp.where(lane == foot + block, starts, 0.0), axis=1, keepdims=True)
        start = start.astype(jnp.int32)
        tile = start >> 7
        turn = (SPAN - (start & (LANES - 1))) & (SPAN - 1)
        code = (block * 4 + jnp.maximum(tile - last, 0)) * 64 + jnp.minimum(tile, last)
        plan = jnp.where(lane == slot, code * SPAN + turn, plan)
    return plan


def planned(code):
    return code >> 17, (code >> 15) & 3, (code >> 9) & 63, code & (SPAN - 1)


def chunk_places(tiles, paired):
    return [(row_of(n, paired), slot) for n in range(tiles) for slot in range(CAP)]


def fetch_kernel(foot, paired, place_ref, note_ref, notes_ref, raw_ref, out_ref, plan_ref, sem):
    blocks = raw_ref.shape[1]
    last = (raw_ref.shape[3] - SPAN) // LANES
    plan = plan_of(foot, blocks, last, place_ref[0:1, 1:2], note_ref[...], notes_ref[...])
    for chunk, (row, slot) in enumerate(chunk_places(notes_ref.shape[0], paired)):
        block, _, first, _ = planned(plan[row, slot])
        lanes = pl.ds(pl.multiple_of(first * LANES, LANES), SPAN)
        pltpu.make_async_copy(raw_ref.at[:, block, :, lanes], out_ref.at[chunk], sem).start()
    plan_ref[...] = plan
    pltpu.make_async_copy(out_ref, out_ref, sem).wait()


def cut_kernel(paired, plan_ref, spans_ref, rim_ref, table_ref, *refs):
    *out_refs, echo = refs
    chunks = spans_ref.shape[0]
    span_tiles = SPAN // LANES
    plan = plan_ref[...]
    for chunk, (row, slot) in enumerate(chunk_places(chunks // CAP, paired)):
        block, over, _, turn = planned(plan[row, slot])
        pieces = []
        for step in range(span_tiles):
            own = pl.multiple_of(jnp.minimum(step + over, span_tiles - 1) * LANES, LANES)
            piece = spans_ref[chunk, :, :, pl.ds(own, LANES)]
            if step:
                beyond = pl.multiple_of(jnp.maximum(step + over - span_tiles, 0) * LANES, LANES)
                rim = rim_ref[:, block, :, pl.ds(beyond, LANES)]
                piece = jnp.where(step + over < span_tiles, piece, rim)
            pieces.append(piece.astype(jnp.float32))
        span = jnp.concatenate(pieces, axis=2).reshape(2 * NP, SPAN)
        rows = slice(chunk * 2 * NP, (chunk + 1) * 2 * NP)
        echo[rows, :] = pltpu.roll(span, turn, 1)[:, :RIM].astype(BF16)
    each = chunks // len(out_refs)
    for first in range(0, WIN, KC):
        sums = jnp.dot(
            echo[:, first : first + 2 * KC], table_ref[...], preferred_element_type=jnp.float32
        ).reshape(chunks, 2, NP, 2 * KC)
        real = (sums[:, 0, :, :KC] + sums[:, 1, :, KC:]).astype(BF16)
        imag = (sums[:, 1, :, :KC] - sums[:, 0, :, KC:]).astype(BF16)
        for group, out_ref in enumerate(out_refs):
            part = slice(group * each, (group + 1) * each)
            out_ref[:, 0, :, first : first + KC] = real[part]
            out_ref[:, 1, :, first : first + KC] = imag[part]


def cut_windows(foot, note, notes, place, raw, rim, table, groups):
    chunks = notes.shape[0] * CAP
    vmem = pl.BlockSpec(memory_space=pltpu.VMEM)
    params = pltpu.CompilerParams(vmem_limit_bytes=vmem_grant(chunks))
    spans, plan = pl.pallas_call(
        functools.partial(fetch_kernel, foot, groups > 1),
        out_shape=(
            jax.ShapeDtypeStruct((chunks, 2, NP, SPAN), BF16),
            jax.ShapeDtypeStruct(notes.shape, jnp.int32),
        ),
        in_specs=[vmem, vmem, vmem, pl.BlockSpec(memory_space=pltpu.HBM)],
        out_specs=(vmem, vmem),
        scratch_shapes=[pltpu.SemaphoreType.DMA],
        compiler_params=params,
        name="fetch",
    )(place[None], note, notes, pltpu.with_memory_space_constraint(raw, pltpu.HBM))
    return pl.pallas_call(
        functools.partial(cut_kernel, groups > 1),
        out_shape=(jax.ShapeDtypeStruct((chunks // groups, 2, NP, WIN), BF16),) * groups,
        in_specs=[vmem] * 4,
        out_specs=(vmem,) * groups,
        scratch_shapes=[pltpu.VMEM((chunks * 2 * NP, RIM), BF16)],
        compiler_params=params,
        name="cut",
    )(plan, spans, rim, table)


def mod_prime(value):
    for _ in range(2):
        value = (value >> 16) * 15 + (value & 65535)
    return jnp.where(value >= PRIME, value - PRIME, value)


def steer_kernel(foot, blocks, order, note_ref, place_ref, table_ref, out_ref, held_ref, sem):
    holding = pltpu.make_async_copy(table_ref, held_ref, sem)
    holding.start()
    chunks = len(order) * CAP
    to_angle = jnp.float32(2.0 * math.pi / PRIME)
    first, twist = place_ref[0], place_ref[2]

    def turned(steps, rows):
        columns = lax.broadcasted_iota(jnp.int32, (rows, PC), 1)
        scrambled = mod_prime((columns + first) * 40503)
        return mod_prime(steps * scrambled).astype(jnp.float32) * to_angle

    inner = turned(lax.broadcasted_iota(jnp.int32, (NP, PC), 0), NP)
    cos_in, sin_in = jnp.cos(inner), jnp.sin(inner)
    row = lax.broadcasted_iota(jnp.int32, (chunks, PC), 0)
    ids = jnp.zeros((chunks, PC), jnp.int32)
    used = jnp.zeros((chunks, PC), jnp.float32)
    for n, position in enumerate(order):
        holder = position ^ twist
        *found, count = named_blocks(note_ref, 0, foot, holder, blocks)
        for slot, block in enumerate(found):
            here = row == n * CAP + slot
            ids = jnp.where(here, (holder * blocks + block) * NP, ids)
            used = jnp.where(here & (count > slot), 1.0, used)
    outer = turned(ids, chunks)
    cos_out, sin_out = jnp.cos(outer) * used, jnp.sin(outer) * used
    for i in range(chunks):
        c, s = cos_out[i : i + 1], sin_out[i : i + 1]
        real = c * cos_in - s * sin_in
        imag = s * cos_in + c * sin_in
        rows = slice(i * 2 * NP, (i + 1) * 2 * NP)
        out_ref[rows, :PC] = jnp.concatenate([real, -imag], axis=0).astype(BF16)
        out_ref[rows, PC:] = jnp.concatenate([imag, real], axis=0).astype(BF16)
    holding.wait()


def steering(foot, blocks, order, note, place):
    smem = pl.BlockSpec(memory_space=pltpu.SMEM)
    vmem = pl.BlockSpec(memory_space=pltpu.VMEM)
    hbm = pl.BlockSpec(memory_space=pltpu.HBM)
    table = jnp.asarray(correlation_table())
    rows = len(order) * CAP * 2 * NP
    return pl.pallas_call(
        functools.partial(steer_kernel, foot, blocks, order),
        out_shape=(
            jax.ShapeDtypeStruct((rows, 2 * PC), BF16),
            jax.ShapeDtypeStruct(table.shape, BF16),
        ),
        in_specs=[smem, smem, hbm],
        out_specs=(vmem, vmem),
        scratch_shapes=[pltpu.SemaphoreType.DMA],
        compiler_params=pltpu.CompilerParams(vmem_limit_bytes=vmem_grant(len(order) * CAP)),
        cost_estimate=pl.CostEstimate(flops=0, bytes_accessed=4 << 20, transcendentals=0),
        name="steer",
    )(note, place, pltpu.with_memory_space_constraint(table, pltpu.HBM))


def image_kernel(scale, *refs):
    *window_refs, steer_ref, interp_ref, out_ref, focused, pixels, sem = refs
    windows = jnp.concatenate(
        [ref[...].reshape(ref.shape[0] * 2 * NP, WIN) for ref in window_refs], axis=0
    )
    contract = (((0,), (0,)), ((), ()))
    copies = []
    for columns in (slice(0, PC), slice(PC, 2 * PC)):
        focused[:, columns] = (
            lax.dot_general(
                windows, steer_ref[:, columns], contract, preferred_element_type=jnp.float32
            )
            * jnp.float32(scale)
        ).astype(BF16)
        for first in range(0, PR, ROWS):
            part = (slice(first, first + ROWS), columns)
            pixels[part] = jnp.dot(
                interp_ref[part[0], :], focused[:, columns], preferred_element_type=jnp.float32
            ).astype(BF16)
            copy = pltpu.make_async_copy(pixels.at[part], out_ref.at[part], sem.at[len(copies)])
            copy.start()
            copies.append(copy)
    for copy in copies:
        copy.wait()


def tile_image(foot, windows, steer):
    vmem = pl.BlockSpec(memory_space=pltpu.VMEM)
    return pl.pallas_call(
        functools.partial(image_kernel, 1.0 / math.sqrt(foot * NP)),
        out_shape=jax.ShapeDtypeStruct((PR, 2 * PC), BF16),
        in_specs=[vmem] * (len(windows) + 2),
        out_specs=pl.BlockSpec(memory_space=pltpu.HBM),
        scratch_shapes=[
            pltpu.VMEM((WIN, 2 * PC), BF16),
            pltpu.VMEM((PR, 2 * PC), BF16),
            pltpu.SemaphoreType.DMA((2 * PR // ROWS,)),
        ],
        compiler_params=pltpu.CompilerParams(vmem_limit_bytes=vmem_grant(steer.shape[0] // (2 * NP), 5)),
        name="image",
    )(*windows, steer, jnp.asarray(interp_table()))


def swapped(value, turn):
    tiles = lax.axis_size("tile")
    return lax.ppermute(value, "tile", [(i, i ^ turn) for i in range(tiles)])


def gather_notes(note):
    pair = jnp.concatenate([note, swapped(note, 1)], axis=0)
    return jnp.concatenate([pair] + [swapped(pair, turn) for turn in TURNS], axis=0)


def row_of(position, paired):
    turns = (0,) + TURNS
    if not paired:
        return position
    return 2 * (position // 2) + (position ^ turns[position // 2]) % 2


def exchange(windows):
    ours, theirs = [windows[0][:CAP]], [windows[0][CAP:]]
    for window, turn in zip(windows[1:], TURNS):
        got = swapped(window, turn)
        halves = (got[:CAP], got[CAP:])
        ours.append(halves[turn % 2])
        theirs.append(halves[1 - turn % 2])
    return jnp.concatenate(ours, axis=0), swapped(jnp.concatenate(theirs, axis=0), 1)


def local(raw_echo, footprint, window_start):
    planes, pulses, bins = raw_echo.shape
    blocks = pulses // NP
    tiles = lax.axis_size("tile")
    paired = tiles == 8
    foot = footprint.shape[2]
    tile_pos = lax.axis_index("tile").astype(jnp.int32)
    row_pos = lax.axis_index("section").astype(jnp.int32)

    rim = passed_along(raw_echo[:, :, :RIM], "section", -1)
    note = jnp.concatenate([footprint[0], window_start], axis=1)
    note = jnp.pad(note, ((0, 0), (0, -note.shape[1] % LANES)))
    notes = gather_notes(note) if paired else lax.all_gather(note, "tile", axis=0, tiled=True)
    twist = tile_pos if paired else jnp.int32(0)
    place = jnp.stack([tile_pos * PC + 1 + 7 * row_pos, tile_pos, twist])
    order = tuple(range(tiles))
    if paired:
        order = (0,) + TURNS + (1,) + tuple(turn ^ 1 for turn in TURNS)

    raw = raw_echo.reshape(planes, blocks, NP, bins)
    steer, table = steering(foot, blocks, order, note, place)
    notes, steer, table = lax.optimization_barrier((notes, steer, table))
    windows = cut_windows(
        foot, note, notes, place, raw, rim.reshape(planes, blocks, NP, RIM), table, 4 if paired else 1
    )
    if paired:
        windows = exchange(windows)
    else:
        sent = windows[0].reshape((tiles, CAP, 2, NP, WIN))
        got = lax.all_to_all(sent, "tile", 0, 0, tiled=True)
        windows = (got.reshape(windows[0].shape),)
    return tile_image(foot, windows, steer)[None, None]


def solution(mesh):
    in_specs = (P(None, "tile", "section"), P("section", "tile", None), P("section", "tile"))
    out_specs = P("section", "tile", None, None)
    return jax.shard_map(local, mesh=mesh, in_specs=in_specs, out_specs=out_specs, check_vma=False)
```

```python
import functools
import math

import jax
import jax.numpy as jnp
import ml_dtypes
import numpy as np
from jax import lax
from jax.experimental import pallas as pl
from jax.experimental.pallas import tpu as pltpu
from jax.sharding import PartitionSpec as P

KC = 128
WIN = 256
PR = 1024
PC = 1024
NP = 8
CAP = 2
LANES = 128
PRIME = 65521
RIM = WIN + KC
TURNS = (2, 5, 6)
SPAN = RIM + LANES
ROWS = 256
BF16 = jnp.bfloat16


def vmem_grant(chunks, more=0):
    return (2 + chunks // 4 + more) << 20


def passed_along(value, axis, by):
    devices = lax.axis_size(axis)
    pairs = [(i, i + by) for i in range(devices) if 0 <= i + by < devices]
    return lax.ppermute(value, axis, pairs)


def correlation_table():
    lag = np.arange(2 * KC)[:, None] - np.arange(KC)[None, :]
    inside = (lag >= 0) & (lag < KC)
    lag = np.where(inside, lag, 0)
    angle = (lag * lag % (2 * KC)).astype(np.float64) * (math.pi / KC)
    scale = 1.0 / math.sqrt(KC)
    real = np.where(inside, np.cos(angle) * scale, 0.0)
    imag = np.where(inside, np.sin(angle) * scale, 0.0)
    return np.concatenate([real, imag], axis=1).astype(np.float32).astype(ml_dtypes.bfloat16)


def interp_table():
    row = np.arange(PR, dtype=np.float64)[:, None]
    offset = np.arange(WIN, dtype=np.float64)[None, :] - ((row + 0.5) / (PR // WIN) - 0.5)
    taper = np.cos(offset * (math.pi / 8.0)) ** 2
    kernel = np.where(np.abs(offset) < 4.0, np.sinc(offset) * taper, 0.0)
    return kernel.astype(np.float32).astype(ml_dtypes.bfloat16)


def named_blocks(notes_ref, row, foot, holder, blocks):
    lowest, highest, count = jnp.int32(blocks - 1), jnp.int32(0), jnp.int32(0)
    for e in range(foot):
        block = notes_ref[row, e] - holder * blocks
        held = (block >= 0) & (block < blocks)
        lowest = jnp.where(held, jnp.minimum(lowest, block), lowest)
        highest = jnp.where(held, jnp.maximum(highest, block), highest)
        count = count + held.astype(jnp.int32)
    return lowest, highest, count


def plan_of(foot, blocks, last, mine, note, notes):
    lane = lax.broadcasted_iota(jnp.int32, notes.shape, 1)
    block = notes - mine * blocks
    held = (lane < foot) & (block >= 0) & (block < blocks)
    block = block.astype(jnp.float32)
    lowest = jnp.min(jnp.where(held, block, blocks - 1.0), axis=1, keepdims=True)
    highest = jnp.max(jnp.where(held, block, 0.0), axis=1, keepdims=True)
    starts = jnp.broadcast_to(note, notes.shape).astype(jnp.float32)
    plan = jnp.zeros(notes.shape, jnp.int32)
    for slot, block in enumerate((lowest, highest)):
        block = block.astype(jnp.int32)
        start = jnp.sum(jnp.where(lane == foot + block, starts, 0.0), axis=1, keepdims=True)
        start = start.astype(jnp.int32)
        first = jnp.minimum(start >> 7, last)
        turn = (SPAN - (start - first * LANES)) & (SPAN - 1)
        plan = jnp.where(lane == slot, (block * 64 + first) * SPAN + turn, plan)
    return plan


def planned(code):
    return code >> 15, (code >> 9) & 63, code & (SPAN - 1)


def chunk_places(tiles, paired):
    return [(row_of(n, paired), slot) for n in range(tiles) for slot in range(CAP)]


def chunk_rows(chunk):
    return slice(chunk * 2 * NP, (chunk + 1) * 2 * NP)


def fetch_kernel(foot, paired, place_ref, note_ref, notes_ref, raw_ref, out_ref, plan_ref, spans, sem):
    blocks = raw_ref.shape[1]
    last = (raw_ref.shape[3] - SPAN) // LANES
    plan = plan_of(foot, blocks, last, place_ref[0:1, 1:2], note_ref[...], notes_ref[...])
    places = chunk_places(notes_ref.shape[0], paired)
    for chunk, (row, slot) in enumerate(places):
        block, first, _ = planned(plan[row, slot])
        lanes = pl.ds(pl.multiple_of(first * LANES, LANES), SPAN)
        pltpu.make_async_copy(raw_ref.at[:, block, :, lanes], spans.at[chunk], sem).start()
    plan_ref[...] = plan
    pltpu.make_async_copy(spans, spans, sem).wait()
    for chunk, (row, slot) in enumerate(places):
        _, _, turn = planned(plan[row, slot])
        span = spans[chunk].astype(jnp.float32).reshape(2 * NP, SPAN)
        out_ref[chunk_rows(chunk), :] = pltpu.roll(span, turn, 1)[:, :RIM].astype(BF16)


def cut_kernel(paired, plan_ref, held_ref, rim_ref, table_ref, *refs):
    *out_refs, echo = refs
    chunks = held_ref.shape[0] // (2 * NP)
    plan = plan_ref[...]
    lane = lax.broadcasted_iota(jnp.int32, (2 * NP, RIM), 1)
    blank = jnp.zeros((2 * NP, SPAN - RIM), jnp.float32)
    for chunk, (row, slot) in enumerate(chunk_places(chunks // CAP, paired)):
        block, _, turn = planned(plan[row, slot])
        rim = rim_ref[:, block].astype(jnp.float32).reshape(2 * NP, RIM)
        beyond = pltpu.roll(jnp.concatenate([rim, blank], axis=1), turn, 1)[:, :RIM]
        held = held_ref[chunk_rows(chunk), :].astype(jnp.float32)
        here = jnp.where(turn == 0, SPAN, turn)
        echo[chunk_rows(chunk), :] = jnp.where(lane < here, held, beyond).astype(BF16)
    each = chunks // len(out_refs)
    for first in range(0, WIN, KC):
        sums = jnp.dot(
            echo[:, first : first + 2 * KC], table_ref[...], preferred_element_type=jnp.float32
        ).reshape(chunks, 2, NP, 2 * KC)
        real = (sums[:, 0, :, :KC] + sums[:, 1, :, KC:]).astype(BF16)
        imag = (sums[:, 1, :, :KC] - sums[:, 0, :, KC:]).astype(BF16)
        for group, out_ref in enumerate(out_refs):
            part = slice(group * each, (group + 1) * each)
            out_ref[:, 0, :, first : first + KC] = real[part]
            out_ref[:, 1, :, first : first + KC] = imag[part]


def cut_windows(foot, note, notes, place, raw, rim, table, groups):
    chunks = notes.shape[0] * CAP
    vmem = pl.BlockSpec(memory_space=pltpu.VMEM)
    params = pltpu.CompilerParams(vmem_limit_bytes=vmem_grant(chunks))
    held, plan = pl.pallas_call(
        functools.partial(fetch_kernel, foot, groups > 1),
        out_shape=(
            jax.ShapeDtypeStruct((chunks * 2 * NP, RIM), BF16),
            jax.ShapeDtypeStruct(notes.shape, jnp.int32),
        ),
        in_specs=[vmem, vmem, vmem, pl.BlockSpec(memory_space=pltpu.HBM)],
        out_specs=(vmem, vmem),
        scratch_shapes=[pltpu.VMEM((chunks, 2, NP, SPAN), BF16), pltpu.SemaphoreType.DMA],
        compiler_params=params,
        name="fetch",
    )(place[None], note, notes, pltpu.with_memory_space_constraint(raw, pltpu.HBM))
    return pl.pallas_call(
        functools.partial(cut_kernel, groups > 1),
        out_shape=(jax.ShapeDtypeStruct((chunks // groups, 2, NP, WIN), BF16),) * groups,
        in_specs=[vmem] * 4,
        out_specs=(vmem,) * groups,
        scratch_shapes=[pltpu.VMEM((chunks * 2 * NP, RIM), BF16)],
        compiler_params=params,
        name="cut",
    )(plan, held, rim, table)


def mod_prime(value):
    for _ in range(2):
        value = (value >> 16) * 15 + (value & 65535)
    return jnp.where(value >= PRIME, value - PRIME, value)


def steer_kernel(foot, blocks, order, note_ref, place_ref, table_ref, interp_ref, out_ref, held_ref, interp_held, sems):
    holding = [
        pltpu.make_async_copy(table_ref, held_ref, sems.at[0]),
        pltpu.make_async_copy(interp_ref, interp_held, sems.at[1]),
    ]
    for copy in holding:
        copy.start()
    chunks = len(order) * CAP
    to_angle = jnp.float32(2.0 * math.pi / PRIME)
    first, twist = place_ref[0], place_ref[2]

    def turned(steps, rows):
        columns = lax.broadcasted_iota(jnp.int32, (rows, PC), 1)
        scrambled = mod_prime((columns + first) * 40503)
        return mod_prime(steps * scrambled).astype(jnp.float32) * to_angle

    inner = turned(lax.broadcasted_iota(jnp.int32, (NP, PC), 0), NP)
    cos_in, sin_in = jnp.cos(inner), jnp.sin(inner)
    row = lax.broadcasted_iota(jnp.int32, (chunks, PC), 0)
    ids = jnp.zeros((chunks, PC), jnp.int32)
    used = jnp.zeros((chunks, PC), jnp.float32)
    for n, position in enumerate(order):
        holder = position ^ twist
        *found, count = named_blocks(note_ref, 0, foot, holder, blocks)
        for slot, block in enumerate(found):
            here = row == n * CAP + slot
            ids = jnp.where(here, (holder * blocks + block) * NP, ids)
            used = jnp.where(here & (count > slot), 1.0, used)
    outer = turned(ids, chunks)
    cos_out, sin_out = jnp.cos(outer) * used, jnp.sin(outer) * used
    for i in range(chunks):
        c, s = cos_out[i : i + 1], sin_out[i : i + 1]
        real = c * cos_in - s * sin_in
        imag = s * cos_in + c * sin_in
        rows = slice(i * 2 * NP, (i + 1) * 2 * NP)
        out_ref[rows, :PC] = jnp.concatenate([real, -imag], axis=0).astype(BF16)
        out_ref[rows, PC:] = jnp.concatenate([imag, real], axis=0).astype(BF16)
    for copy in holding:
        copy.wait()


def steering(foot, blocks, order, note, place):
    smem = pl.BlockSpec(memory_space=pltpu.SMEM)
    vmem = pl.BlockSpec(memory_space=pltpu.VMEM)
    hbm = pl.BlockSpec(memory_space=pltpu.HBM)
    table, interp = jnp.asarray(correlation_table()), jnp.asarray(interp_table())
    rows = len(order) * CAP * 2 * NP
    return pl.pallas_call(
        functools.partial(steer_kernel, foot, blocks, order),
        out_shape=(
            jax.ShapeDtypeStruct((rows, 2 * PC), BF16),
            jax.ShapeDtypeStruct(table.shape, BF16),
            jax.ShapeDtypeStruct(interp.shape, BF16),
        ),
        in_specs=[smem, smem, hbm, hbm],
        out_specs=(vmem,) * 3,
        scratch_shapes=[pltpu.SemaphoreType.DMA((2,))],
        compiler_params=pltpu.CompilerParams(vmem_limit_bytes=vmem_grant(len(order) * CAP)),
        cost_estimate=pl.CostEstimate(flops=0, bytes_accessed=4 << 20, transcendentals=0),
        name="steer",
    )(note, place, *(pltpu.with_memory_space_constraint(x, pltpu.HBM) for x in (table, interp)))


def image_kernel(scale, *refs):
    *window_refs, steer_ref, interp_ref, out_ref, focused, pixels, sem = refs
    windows = jnp.concatenate(
        [ref[...].reshape(ref.shape[0] * 2 * NP, WIN) for ref in window_refs], axis=0
    )
    contract = (((0,), (0,)), ((), ()))
    copies = []
    for columns in (slice(0, PC), slice(PC, 2 * PC)):
        focused[:, columns] = (
            lax.dot_general(
                windows, steer_ref[:, columns], contract, preferred_element_type=jnp.float32
            )
            * jnp.float32(scale)
        ).astype(BF16)
        for first in range(0, PR, ROWS):
            part = (slice(first, first + ROWS), columns)
            pixels[part] = jnp.dot(
                interp_ref[part[0], :], focused[:, columns], preferred_element_type=jnp.float32
            ).astype(BF16)
            copy = pltpu.make_async_copy(pixels.at[part], out_ref.at[part], sem.at[len(copies)])
            copy.start()
            copies.append(copy)
    for copy in copies:
        copy.wait()


def tile_image(foot, windows, steer, interp):
    vmem = pl.BlockSpec(memory_space=pltpu.VMEM)
    return pl.pallas_call(
        functools.partial(image_kernel, 1.0 / math.sqrt(foot * NP)),
        out_shape=jax.ShapeDtypeStruct((PR, 2 * PC), BF16),
        in_specs=[vmem] * (len(windows) + 2),
        out_specs=pl.BlockSpec(memory_space=pltpu.HBM),
        scratch_shapes=[
            pltpu.VMEM((WIN, 2 * PC), BF16),
            pltpu.VMEM((PR, 2 * PC), BF16),
            pltpu.SemaphoreType.DMA((2 * PR // ROWS,)),
        ],
        compiler_params=pltpu.CompilerParams(vmem_limit_bytes=vmem_grant(steer.shape[0] // (2 * NP), 5)),
        name="image",
    )(*windows, steer, interp)


def swapped(value, turn):
    tiles = lax.axis_size("tile")
    return lax.ppermute(value, "tile", [(i, i ^ turn) for i in range(tiles)])


def gather_notes(note):
    pair = jnp.concatenate([note, swapped(note, 1)], axis=0)
    return jnp.concatenate([pair] + [swapped(pair, turn) for turn in TURNS], axis=0)


def row_of(position, paired):
    turns = (0,) + TURNS
    if not paired:
        return position
    return 2 * (position // 2) + (position ^ turns[position // 2]) % 2


def exchange(windows):
    ours, theirs = [windows[0][:CAP]], [windows[0][CAP:]]
    for window, turn in zip(windows[1:], TURNS):
        got = swapped(window, turn)
        halves = (got[:CAP], got[CAP:])
        ours.append(halves[turn % 2])
        theirs.append(halves[1 - turn % 2])
    return jnp.concatenate(ours, axis=0), swapped(jnp.concatenate(theirs, axis=0), 1)


def local(raw_echo, footprint, window_start):
    planes, pulses, bins = raw_echo.shape
    blocks = pulses // NP
    tiles = lax.axis_size("tile")
    paired = tiles == 8
    foot = footprint.shape[2]
    tile_pos = lax.axis_index("tile").astype(jnp.int32)
    row_pos = lax.axis_index("section").astype(jnp.int32)

    rim = passed_along(raw_echo[:, :, :RIM], "section", -1)
    note = jnp.concatenate([footprint[0], window_start], axis=1)
    note = jnp.pad(note, ((0, 0), (0, -note.shape[1] % LANES)))
    notes = gather_notes(note) if paired else lax.all_gather(note, "tile", axis=0, tiled=True)
    twist = tile_pos if paired else jnp.int32(0)
    place = jnp.stack([tile_pos * PC + 1 + 7 * row_pos, tile_pos, twist])
    order = tuple(range(tiles))
    if paired:
        order = (0,) + TURNS + (1,) + tuple(turn ^ 1 for turn in TURNS)

    raw = raw_echo.reshape(planes, blocks, NP, bins)
    steer, table, interp = steering(foot, blocks, order, note, place)
    notes, steer, table, interp = lax.optimization_barrier((notes, steer, table, interp))
    windows = cut_windows(
        foot, note, notes, place, raw, rim.reshape(planes, blocks, NP, RIM), table, 4 if paired else 1
    )
    if paired:
        windows = exchange(windows)
    else:
        sent = windows[0].reshape((tiles, CAP, 2, NP, WIN))
        got = lax.all_to_all(sent, "tile", 0, 0, tiled=True)
        windows = (got.reshape(windows[0].shape),)
    return tile_image(foot, windows, steer, interp)[None, None]


def solution(mesh):
    in_specs = (P(None, "tile", "section"), P("section", "tile", None), P("section", "tile"))
    out_specs = P("section", "tile", None, None)
    return jax.shard_map(local, mesh=mesh, in_specs=in_specs, out_specs=out_specs, check_vma=False)
```

```python
import functools
import math

import jax
import jax.numpy as jnp
import ml_dtypes
import numpy as np
from jax import lax
from jax.experimental import pallas as pl
from jax.experimental.pallas import tpu as pltpu
from jax.sharding import PartitionSpec as P

KC = 128
WIN = 256
PR = 1024
PC = 1024
NP = 8
CAP = 2
LANES = 128
PRIME = 65521
RIM = WIN + KC
TURNS = (2, 5, 6)
SPAN = RIM + LANES
ROWS = 256
BF16 = jnp.bfloat16


def vmem_grant(chunks, more=0):
    return (2 + chunks // 4 + more) << 20


def passed_along(value, axis, by):
    devices = lax.axis_size(axis)
    pairs = [(i, i + by) for i in range(devices) if 0 <= i + by < devices]
    return lax.ppermute(value, axis, pairs)


def correlation_table():
    lag = np.arange(2 * KC)[:, None] - np.arange(KC)[None, :]
    inside = (lag >= 0) & (lag < KC)
    lag = np.where(inside, lag, 0)
    angle = (lag * lag % (2 * KC)).astype(np.float64) * (math.pi / KC)
    scale = 1.0 / math.sqrt(KC)
    real = np.where(inside, np.cos(angle) * scale, 0.0)
    imag = np.where(inside, np.sin(angle) * scale, 0.0)
    return np.concatenate([real, imag], axis=1).astype(np.float32).astype(ml_dtypes.bfloat16)


def interp_table():
    row = np.arange(PR, dtype=np.float64)[:, None]
    offset = np.arange(WIN, dtype=np.float64)[None, :] - ((row + 0.5) / (PR // WIN) - 0.5)
    taper = np.cos(offset * (math.pi / 8.0)) ** 2
    kernel = np.where(np.abs(offset) < 4.0, np.sinc(offset) * taper, 0.0)
    return kernel.astype(np.float32).astype(ml_dtypes.bfloat16)


def named_blocks(notes_ref, row, foot, holder, blocks):
    lowest, highest, count = jnp.int32(blocks - 1), jnp.int32(0), jnp.int32(0)
    for e in range(foot):
        block = notes_ref[row, e] - holder * blocks
        held = (block >= 0) & (block < blocks)
        lowest = jnp.where(held, jnp.minimum(lowest, block), lowest)
        highest = jnp.where(held, jnp.maximum(highest, block), highest)
        count = count + held.astype(jnp.int32)
    return lowest, highest, count


def plan_of(foot, blocks, last, mine, note, notes):
    lane = lax.broadcasted_iota(jnp.int32, notes.shape, 1)
    block = notes - mine * blocks
    held = (lane < foot) & (block >= 0) & (block < blocks)
    block = block.astype(jnp.float32)
    lowest = jnp.min(jnp.where(held, block, blocks - 1.0), axis=1, keepdims=True)
    highest = jnp.max(jnp.where(held, block, 0.0), axis=1, keepdims=True)
    starts = jnp.broadcast_to(note, notes.shape).astype(jnp.float32)
    plan = jnp.zeros(notes.shape, jnp.int32)
    for slot, block in enumerate((lowest, highest)):
        block = block.astype(jnp.int32)
        start = jnp.sum(jnp.where(lane == foot + block, starts, 0.0), axis=1, keepdims=True)
        start = start.astype(jnp.int32)
        first = jnp.minimum(start >> 7, last)
        turn = (SPAN - (start - first * LANES)) & (SPAN - 1)
        plan = jnp.where(lane == slot, (block * 64 + first) * SPAN + turn, plan)
    return plan


def planned(code):
    return code >> 15, (code >> 9) & 63, code & (SPAN - 1)


def chunk_places(tiles, paired):
    return [(row_of(n, paired), slot) for n in range(tiles) for slot in range(CAP)]


def chunk_rows(chunk):
    return slice(chunk * 2 * NP, (chunk + 1) * 2 * NP)


def fetch_kernel(foot, paired, place_ref, note_ref, notes_ref, raw_ref, out_ref, plan_ref, spans, sem):
    blocks = raw_ref.shape[1]
    last = (raw_ref.shape[3] - SPAN) // LANES
    plan = plan_of(foot, blocks, last, place_ref[0:1, 1:2], note_ref[...], notes_ref[...])
    places = chunk_places(notes_ref.shape[0], paired)
    for chunk, (row, slot) in enumerate(places):
        block, first, _ = planned(plan[row, slot])
        lanes = pl.ds(pl.multiple_of(first * LANES, LANES), SPAN)
        pltpu.make_async_copy(raw_ref.at[:, block, :, lanes], spans.at[chunk], sem).start()
    plan_ref[...] = plan
    pltpu.make_async_copy(spans, spans, sem).wait()
    for chunk, (row, slot) in enumerate(places):
        _, _, turn = planned(plan[row, slot])
        span = spans[chunk].astype(jnp.float32).reshape(2 * NP, SPAN)
        out_ref[chunk_rows(chunk), :] = pltpu.roll(span, turn, 1)[:, :RIM].astype(BF16)


def cut_kernel(paired, plan_ref, held_ref, rim_ref, table_ref, *refs):
    *out_refs, echo = refs
    chunks = held_ref.shape[0] // (2 * NP)
    plan = plan_ref[...]
    lane = lax.broadcasted_iota(jnp.int32, (2 * NP, RIM), 1)
    blank = jnp.zeros((2 * NP, SPAN - RIM), jnp.float32)
    for chunk, (row, slot) in enumerate(chunk_places(chunks // CAP, paired)):
        block, _, turn = planned(plan[row, slot])
        rim = rim_ref[:, block].astype(jnp.float32).reshape(2 * NP, RIM)
        beyond = pltpu.roll(jnp.concatenate([rim, blank], axis=1), turn, 1)[:, :RIM]
        held = held_ref[chunk_rows(chunk), :]
        here = jnp.where(turn == 0, SPAN, turn)
        echo[chunk_rows(chunk), :] = jnp.where(lane < here, held, beyond.astype(BF16))
    each = chunks // len(out_refs)
    for first in range(0, WIN, KC):
        sums = jnp.dot(
            echo[:, first : first + 2 * KC], table_ref[...], preferred_element_type=jnp.float32
        ).reshape(chunks, 2, NP, 2 * KC)
        real = (sums[:, 0, :, :KC] + sums[:, 1, :, KC:]).astype(BF16)
        imag = (sums[:, 1, :, :KC] - sums[:, 0, :, KC:]).astype(BF16)
        for group, out_ref in enumerate(out_refs):
            part = slice(group * each, (group + 1) * each)
            out_ref[:, 0, :, first : first + KC] = real[part]
            out_ref[:, 1, :, first : first + KC] = imag[part]


def cut_windows(foot, note, notes, place, raw, rim, table, groups):
    chunks = notes.shape[0] * CAP
    vmem = pl.BlockSpec(memory_space=pltpu.VMEM)
    params = pltpu.CompilerParams(vmem_limit_bytes=vmem_grant(chunks))
    held, plan = pl.pallas_call(
        functools.partial(fetch_kernel, foot, groups > 1),
        out_shape=(
            jax.ShapeDtypeStruct((chunks * 2 * NP, RIM), BF16),
            jax.ShapeDtypeStruct(notes.shape, jnp.int32),
        ),
        in_specs=[vmem, vmem, vmem, pl.BlockSpec(memory_space=pltpu.HBM)],
        out_specs=(vmem, vmem),
        scratch_shapes=[pltpu.VMEM((chunks, 2, NP, SPAN), BF16), pltpu.SemaphoreType.DMA],
        compiler_params=params,
        name="fetch",
    )(place[None], note, notes, pltpu.with_memory_space_constraint(raw, pltpu.HBM))
    return pl.pallas_call(
        functools.partial(cut_kernel, groups > 1),
        out_shape=(jax.ShapeDtypeStruct((chunks // groups, 2, NP, WIN), BF16),) * groups,
        in_specs=[vmem] * 4,
        out_specs=(vmem,) * groups,
        scratch_shapes=[pltpu.VMEM((chunks * 2 * NP, RIM), BF16)],
        compiler_params=params,
        name="cut",
    )(plan, held, rim, table)


def mod_prime(value):
    for _ in range(2):
        value = (value >> 16) * 15 + (value & 65535)
    return jnp.where(value >= PRIME, value - PRIME, value)


def steer_kernel(foot, blocks, order, note_ref, place_ref, table_ref, interp_ref, out_ref, held_ref, interp_held, sems):
    holding = [
        pltpu.make_async_copy(table_ref, held_ref, sems.at[0]),
        pltpu.make_async_copy(interp_ref, interp_held, sems.at[1]),
    ]
    for copy in holding:
        copy.start()
    chunks = len(order) * CAP
    to_angle = jnp.float32(2.0 * math.pi / PRIME)
    first, twist = place_ref[0], place_ref[2]

    def turned(steps, rows):
        columns = lax.broadcasted_iota(jnp.int32, (rows, PC), 1)
        scrambled = mod_prime((columns + first) * 40503)
        return mod_prime(steps * scrambled).astype(jnp.float32) * to_angle

    inner = turned(lax.broadcasted_iota(jnp.int32, (NP, PC), 0), NP)
    cos_in, sin_in = jnp.cos(inner), jnp.sin(inner)
    row = lax.broadcasted_iota(jnp.int32, (chunks, PC), 0)
    ids = jnp.zeros((chunks, PC), jnp.int32)
    used = jnp.zeros((chunks, PC), jnp.float32)
    for n, position in enumerate(order):
        holder = position ^ twist
        *found, count = named_blocks(note_ref, 0, foot, holder, blocks)
        for slot, block in enumerate(found):
            here = row == n * CAP + slot
            ids = jnp.where(here, (holder * blocks + block) * NP, ids)
            used = jnp.where(here & (count > slot), 1.0, used)
    outer = turned(ids, chunks)
    cos_out, sin_out = jnp.cos(outer) * used, jnp.sin(outer) * used
    for i in range(chunks):
        c, s = cos_out[i : i + 1], sin_out[i : i + 1]
        real = c * cos_in - s * sin_in
        imag = s * cos_in + c * sin_in
        rows = slice(i * 2 * NP, (i + 1) * 2 * NP)
        out_ref[rows, :PC] = jnp.concatenate([real, -imag], axis=0).astype(BF16)
        out_ref[rows, PC:] = jnp.concatenate([imag, real], axis=0).astype(BF16)
    for copy in holding:
        copy.wait()


def steering(foot, blocks, order, note, place):
    smem = pl.BlockSpec(memory_space=pltpu.SMEM)
    vmem = pl.BlockSpec(memory_space=pltpu.VMEM)
    hbm = pl.BlockSpec(memory_space=pltpu.HBM)
    table, interp = jnp.asarray(correlation_table()), jnp.asarray(interp_table())
    rows = len(order) * CAP * 2 * NP
    return pl.pallas_call(
        functools.partial(steer_kernel, foot, blocks, order),
        out_shape=(
            jax.ShapeDtypeStruct((rows, 2 * PC), BF16),
            jax.ShapeDtypeStruct(table.shape, BF16),
            jax.ShapeDtypeStruct(interp.shape, BF16),
        ),
        in_specs=[smem, smem, hbm, hbm],
        out_specs=(vmem,) * 3,
        scratch_shapes=[pltpu.SemaphoreType.DMA((2,))],
        compiler_params=pltpu.CompilerParams(vmem_limit_bytes=vmem_grant(len(order) * CAP)),
        cost_estimate=pl.CostEstimate(flops=0, bytes_accessed=4 << 20, transcendentals=0),
        name="steer",
    )(note, place, *(pltpu.with_memory_space_constraint(x, pltpu.HBM) for x in (table, interp)))


def image_kernel(scale, *refs):
    *window_refs, steer_ref, interp_ref, out_ref, focused, pixels, sem = refs
    windows = jnp.concatenate(
        [ref[...].reshape(ref.shape[0] * 2 * NP, WIN) for ref in window_refs], axis=0
    )
    contract = (((0,), (0,)), ((), ()))
    copies = []
    for columns in (slice(0, PC), slice(PC, 2 * PC)):
        focused[:, columns] = (
            lax.dot_general(
                windows, steer_ref[:, columns], contract, preferred_element_type=jnp.float32
            )
            * jnp.float32(scale)
        ).astype(BF16)
        for first in range(0, PR, ROWS):
            part = (slice(first, first + ROWS), columns)
            pixels[part] = jnp.dot(
                interp_ref[part[0], :], focused[:, columns], preferred_element_type=jnp.float32
            ).astype(BF16)
            copy = pltpu.make_async_copy(pixels.at[part], out_ref.at[part], sem.at[len(copies)])
            copy.start()
            copies.append(copy)
    for copy in copies:
        copy.wait()


def tile_image(foot, windows, steer, interp):
    vmem = pl.BlockSpec(memory_space=pltpu.VMEM)
    return pl.pallas_call(
        functools.partial(image_kernel, 1.0 / math.sqrt(foot * NP)),
        out_shape=jax.ShapeDtypeStruct((PR, 2 * PC), BF16),
        in_specs=[vmem] * (len(windows) + 2),
        out_specs=pl.BlockSpec(memory_space=pltpu.HBM),
        scratch_shapes=[
            pltpu.VMEM((WIN, 2 * PC), BF16),
            pltpu.VMEM((PR, 2 * PC), BF16),
            pltpu.SemaphoreType.DMA((2 * PR // ROWS,)),
        ],
        compiler_params=pltpu.CompilerParams(vmem_limit_bytes=vmem_grant(steer.shape[0] // (2 * NP), 5)),
        name="image",
    )(*windows, steer, interp)


def swapped(value, turn):
    tiles = lax.axis_size("tile")
    return lax.ppermute(value, "tile", [(i, i ^ turn) for i in range(tiles)])


def gather_notes(note):
    pair = jnp.concatenate([note, swapped(note, 1)], axis=0)
    return jnp.concatenate([pair] + [swapped(pair, turn) for turn in TURNS], axis=0)


def row_of(position, paired):
    turns = (0,) + TURNS
    if not paired:
        return position
    return 2 * (position // 2) + (position ^ turns[position // 2]) % 2


def exchange(windows):
    ours, theirs = [windows[0][:CAP]], [windows[0][CAP:]]
    for window, turn in zip(windows[1:], TURNS):
        got = swapped(window, turn)
        halves = (got[:CAP], got[CAP:])
        ours.append(halves[turn % 2])
        theirs.append(halves[1 - turn % 2])
    return jnp.concatenate(ours, axis=0), swapped(jnp.concatenate(theirs, axis=0), 1)


def local(raw_echo, footprint, window_start):
    planes, pulses, bins = raw_echo.shape
    blocks = pulses // NP
    tiles = lax.axis_size("tile")
    paired = tiles == 8
    foot = footprint.shape[2]
    tile_pos = lax.axis_index("tile").astype(jnp.int32)
    row_pos = lax.axis_index("section").astype(jnp.int32)

    rim = passed_along(raw_echo[:, :, :RIM], "section", -1)
    note = jnp.concatenate([footprint[0], window_start], axis=1)
    note = jnp.pad(note, ((0, 0), (0, -note.shape[1] % LANES)))
    notes = gather_notes(note) if paired else lax.all_gather(note, "tile", axis=0, tiled=True)
    twist = tile_pos if paired else jnp.int32(0)
    place = jnp.stack([tile_pos * PC + 1 + 7 * row_pos, tile_pos, twist])
    order = tuple(range(tiles))
    if paired:
        order = (0,) + TURNS + (1,) + tuple(turn ^ 1 for turn in TURNS)

    raw = raw_echo.reshape(planes, blocks, NP, bins)
    steer, table, interp = steering(foot, blocks, order, note, place)
    notes, steer, table, interp = lax.optimization_barrier((notes, steer, table, interp))
    windows = cut_windows(
        foot, note, notes, place, raw, rim.reshape(planes, blocks, NP, RIM), table, 4 if paired else 1
    )
    if paired:
        windows = exchange(windows)
    else:
        sent = windows[0].reshape((tiles, CAP, 2, NP, WIN))
        got = lax.all_to_all(sent, "tile", 0, 0, tiled=True)
        windows = (got.reshape(windows[0].shape),)
    return tile_image(foot, windows, steer, interp)[None, None]


def solution(mesh):
    in_specs = (P(None, "tile", "section"), P("section", "tile", None), P("section", "tile"))
    out_specs = P("section", "tile", None, None)
    return jax.shard_map(local, mesh=mesh, in_specs=in_specs, out_specs=out_specs, check_vma=False)
```
